256 devices in a mesh: seq: 32 (over y, z), head: 8 (over x, core).
Axes of the slice: x: 4, y: 4, z: 8, core: 2. Of those that a mesh axis runs over, the one named last changes fastest.
Arguments:
- queries: bfloat16 [8192, 32, 128], P('seq', 'head'), may hold values from -42 to 42, as said below
- keys: bfloat16 [8192, 8, 128], P('seq', 'head'), may hold values from -6 to 6
- values: bfloat16 [8192, 8, 128], P('seq', 'head'), may hold values from -6 to 6
- feat_q: bfloat16 [32, 128, 128], P('head'), may hold values from -0.5 to 0.5
- feat_k: bfloat16 [32, 128, 128], P('head'), may hold values from -0.5 to 0.5
- samples: int32 [32], replicated, may hold values from 0 to 1
Outputs:
- student: bfloat16 [8192, 32, 128], P('seq', 'head')
- teacher: float32 [32, 128, 32, 128], P('seq', None, 'head')
- loss: float32 [], replicated
The draws below stay inside these ranges and needn't reach their ends.
Inputs may be any that keep to these rules, and one draw needn't show every extreme that they name: `queries`: query vectors; some may be large multiples of earlier key vectors.
All inputs are finite; a program needn't handle non-finite values.
Results may differ from the reference program's by a relative error of at most 0.009.
Values may be sent and summed in bfloat16 or wider, within the bound.
No kernel may reach another device: no remote copies, remote signals or barrier semaphores. Data moves between devices by JAX's collectives and lax.ppermute only.
A program may use at most 64 MiB of HBM per device.

```python
import jax
import jax.numpy as jnp
from jax import lax

HD = 128
FEAT = 128
QH_DEV = 4
BLOCK = 128
TOK_DEV = 256
LENGTH = 8192
Q_HEADS = 32
KV_HEADS = 8
N_SEQ = 32


def draw_pair(key):
    key_query = jax.random.fold_in(key, 11)
    key_key = jax.random.fold_in(key, 23)
    query_rows = jnp.clip(jax.random.normal(key_query, (LENGTH, Q_HEADS, HD), jnp.float32), -6.0, 6.0)
    key_rows = jnp.clip(jax.random.normal(key_key, (LENGTH, KV_HEADS, HD), jnp.float32), -6.0, 6.0)
    return (query_rows, key_rows)


def draw_queries(key, part):
    query_rows, key_rows = draw_pair(key)
    return query_rows.astype(jnp.bfloat16)


def draw_keys(key, part):
    query_rows, key_rows = draw_pair(key)
    return key_rows.astype(jnp.bfloat16)


def set_ends(drawn, stream_key, least, high):
    dims = drawn.shape
    index_at = [jax.random.randint(jax.random.fold_in(stream_key, axis), (), 0, dims[axis]) for axis in range(len(dims))]
    drawn = drawn.at[tuple(index_at)].set(least)
    longest = dims.index(max(dims))
    index_at[longest] = (index_at[longest] + 1) % dims[longest]
    return drawn.at[tuple(index_at)].set(high)


def shard_levels(own_key, shape, split, low, largest):
    level = 1.0
    for position, parts in split:
        steps = jax.random.uniform(jax.random.fold_in(jax.random.fold_in(own_key, 6), position), (parts,), jnp.float32, low / len(split), largest / len(split))
        level = level * jnp.repeat(jnp.exp(steps), shape[position] // parts).reshape((-1,) + (1,) * (len(shape) - 1 - position))
    return level


def gaussian(own_key, shape, spread, reach, shards=(), kind=jnp.bfloat16):
    drawn = spread * jax.random.normal(own_key, shape, jnp.float32)
    if shards:
        drawn = drawn * shard_levels(own_key, shape, shards, -0.22, 0.18)
    return jnp.clip(drawn, -reach, reach).astype(kind)


def setup_inputs(seed: int = 0) -> dict:
    key_list = jax.random.split(jax.random.key(seed), 7)
    return {
        "queries": draw_queries(jax.random.fold_in(key_list[6], 71), 0),
        "keys": draw_keys(jax.random.fold_in(key_list[6], 71), 0),
        "values": gaussian(key_list[2], (LENGTH, KV_HEADS, HD), 1.0, 6.0, ((0, 32), (1, 8))),
        "feat_q": gaussian(key_list[3], (Q_HEADS, HD, FEAT), HD ** -0.5, 0.5, ((0, 8),)),
        "feat_k": gaussian(key_list[4], (Q_HEADS, HD, FEAT), HD ** -0.5, 0.5, ((0, 8),)),
        "samples": set_ends(jax.random.randint(key_list[5], (N_SEQ,), 0, TOK_DEV // BLOCK), jax.random.fold_in(key_list[5], 1), 0, (TOK_DEV // BLOCK) - 1).astype(jnp.int32),
    }


PRECISE = lax.Precision.HIGHEST

def features(logits):
    return jnp.concatenate([jax.nn.softmax(logits, axis=-1), jax.nn.softmax(-logits, axis=-1)], axis=-1).astype(jnp.bfloat16)

def reference(queries, keys, values, feat_q, feat_k, samples):
    length, head_count, head_width = queries.shape
    kv_group = jnp.arange(head_count) // QH_DEV
    block_count = length // BLOCK
    query_blocks = queries.reshape(block_count, BLOCK, head_count, head_width)
    key_blocks = keys.reshape(block_count, BLOCK, keys.shape[1], head_width)
    value_blocks = values.reshape(block_count, BLOCK, values.shape[1], head_width)
    feat_q32 = feat_q.astype(jnp.float32)
    feat_k32 = feat_k.astype(jnp.float32)
    causal = jnp.arange(BLOCK)[:, None] >= jnp.arange(BLOCK)[None, :]

    def advance(running, inputs):
        kv_state, key_total = running
        query_part, key_part, value_part = inputs
        key_wide = key_part[:, kv_group].astype(jnp.float32)
        value_wide = value_part[:, kv_group].astype(jnp.float32)
        phi_q = features(jnp.einsum('lhd,hdf->lhf', query_part.astype(jnp.float32), feat_q32, precision=PRECISE)).astype(jnp.float32)
        phi_k = features(jnp.einsum('lhd,hdf->lhf', key_wide, feat_k32, precision=PRECISE)).astype(jnp.float32)
        kernel = jnp.einsum('ihf,jhf->hij', phi_q, phi_k, precision=PRECISE)
        kernel = jnp.where(causal[None], kernel, 0.0)
        kernel_low = lax.optimization_barrier(kernel.astype(jnp.bfloat16)).astype(jnp.float32)
        numer = jnp.einsum('hij,jhd->ihd', kernel_low, value_wide, precision=PRECISE)
        numer = numer + jnp.einsum('ihf,hfd->ihd', phi_q, kv_state, precision=PRECISE)
        denom = lax.optimization_barrier(jnp.sum(kernel, axis=2)).T + jnp.einsum('ihf,hf->ih', phi_q, key_total, precision=PRECISE)
        result = (numer / denom[..., None]).astype(jnp.bfloat16)
        kv_state = kv_state + jnp.einsum('jhf,jhd->hfd', phi_k, value_wide, precision=PRECISE)
        key_total = key_total + lax.optimization_barrier(jnp.sum(phi_k, axis=0))
        return ((kv_state, key_total), result)
    start_state = jnp.zeros((head_count, 2 * FEAT, head_width), jnp.float32)
    start_total = jnp.zeros((head_count, 2 * FEAT), jnp.float32)
    ignored, student_blocks = lax.scan(advance, (start_state, start_total), (query_blocks, key_blocks, value_blocks))
    student = student_blocks.reshape(length, head_count, head_width)
    keys32 = keys.astype(jnp.float32)
    values32 = values.astype(jnp.float32)
    inv_root = 1.0 / jnp.sqrt(jnp.float32(head_width))
    key_places = jnp.arange(length)

    def teach(stretch):
        row_first = (stretch * TOK_DEV + samples[stretch] * BLOCK).astype(jnp.int32)
        query_rows = lax.dynamic_slice_in_dim(queries, row_first, BLOCK, 0).astype(jnp.float32)
        query_rows = query_rows.reshape(BLOCK, keys.shape[1], QH_DEV, head_width)
        row_places = row_first + jnp.arange(BLOCK)
        scores = jnp.einsum('bgnd,kgd->gnbk', query_rows, keys32, precision=PRECISE) * inv_root
        live = key_places[None, :] <= row_places[:, None]
        scores = jnp.where(live[None, None], scores, -jnp.inf)
        peak = lax.optimization_barrier(jnp.max(scores, axis=-1, keepdims=True))
        weights = jnp.exp(scores - peak)
        totals = lax.optimization_barrier(jnp.sum(weights, axis=-1))
        rounded = lax.optimization_barrier(weights.astype(jnp.bfloat16)).astype(jnp.float32)
        mixed = jnp.einsum('gnbk,kgd->gnbd', rounded, values32, precision=PRECISE) / totals[..., None]
        mixed = jnp.transpose(mixed, (2, 0, 1, 3)).reshape(BLOCK, head_count, head_width)
        student_rows = lax.dynamic_slice_in_dim(student, row_first, BLOCK, 0).astype(jnp.float32)
        gap = student_rows - mixed
        return (mixed, jnp.sum(gap * gap))
    teacher, squares = lax.map(teach, jnp.arange(samples.shape[0]).astype(jnp.int32))
    loss = jnp.sum(squares) / (samples.shape[0] * BLOCK * head_count * head_width)
    return (student, teacher, loss)
```

```python
import jax
import jax.numpy as jnp
from jax import lax
from jax.experimental import pallas as pl
from jax.experimental.pallas import tpu as pltpu
from jax.sharding import PartitionSpec as P

HD = 128
FEAT = 128
QH_DEV = 4
BLOCK = 128
MASKED = -1e30
F32 = jnp.float32


def features(logits):
    return jnp.concatenate(
        [jax.nn.softmax(logits, axis=-1), jax.nn.softmax(-logits, axis=-1)], axis=-1
    ).astype(jnp.bfloat16)


def prefix_states(state, total):
    count = lax.axis_size("seq")
    heads, feats, width = state.shape
    rows = heads * feats // count
    parts = jnp.concatenate(
        [
            state.reshape(count, rows, width),
            jnp.pad(total.reshape(count, 1, rows), ((0, 0), (0, 15), (0, width - rows))),
        ],
        axis=1,
    ).astype(jnp.bfloat16)
    mine = lax.all_to_all(parts, "seq", 0, 0)
    earlier = (jnp.arange(count)[:, None] > jnp.arange(count)[None, :]).astype(jnp.bfloat16)
    sums = jnp.einsum("st,trw->srw", earlier, mine, preferred_element_type=F32).astype(jnp.bfloat16)
    back = lax.all_to_all(sums, "seq", 0, 0)
    return (
        back[:, :rows].reshape(heads, feats, width),
        back[:, rows, :rows].reshape(heads, feats),
    )


KEYS_STEP = 1024


def teach_step(place_ref, query_ref, pair_ref, out_ref, best_ref, total_ref, accum_ref):
    step = pl.program_id(0)
    row_first = place_ref[0]
    key_first = step * KEYS_STEP
    rows = query_ref.shape[0]
    width = query_ref.shape[1]

    @pl.when(step == 0)
    def _():
        best_ref[...] = jnp.full(best_ref.shape, MASKED, F32)
        total_ref[...] = jnp.zeros(total_ref.shape, F32)
        accum_ref[...] = jnp.zeros(accum_ref.shape, F32)

    def absorb(masked):
        key_part = pair_ref[:, :width]
        value_part = pair_ref[:, width:]
        scores = lax.dot_general(
            query_ref[...], key_part, (((1,), (1,)), ((), ())), preferred_element_type=F32
        ) * (1.0 / width**0.5)
        if masked:
            place = row_first + lax.rem(lax.broadcasted_iota(jnp.int32, scores.shape, 0), BLOCK)
            live = key_first + lax.broadcasted_iota(jnp.int32, scores.shape, 1) <= place
            scores = jnp.where(live, scores, MASKED)
        best = best_ref[...]
        newtop = jnp.maximum(best, jnp.max(scores, axis=1, keepdims=True))
        fade = jnp.exp(best - newtop)
        weights = jnp.exp(scores - newtop)
        total_ref[...] = fade * total_ref[...] + jnp.sum(weights, axis=1, keepdims=True)
        accum_ref[...] = fade * accum_ref[...] + jnp.dot(
            weights.astype(jnp.bfloat16), value_part, preferred_element_type=F32
        )
        best_ref[...] = newtop

    @pl.when(key_first + KEYS_STEP <= row_first)
    def _():
        absorb(False)

    @pl.when((key_first + KEYS_STEP > row_first) & (key_first <= row_first + BLOCK - 1))
    def _():
        absorb(True)

    @pl.when(step == pl.num_programs(0) - 1)
    def _():
        out_ref[...] = accum_ref[...] / total_ref[...]


def teach(row_first, query_rows, gathered):
    rows, width = query_rows.shape
    return pl.pallas_call(
        teach_step,
        out_shape=jax.ShapeDtypeStruct((rows, width), F32),
        grid_spec=pltpu.PrefetchScalarGridSpec(
            num_scalar_prefetch=1,
            grid=(gathered.shape[0] // KEYS_STEP,),
            in_specs=[
                pl.BlockSpec((rows, width), lambda i, place: (0, 0)),
                pl.BlockSpec((KEYS_STEP, 2 * width), lambda i, place: (i, 0)),
            ],
            out_specs=pl.BlockSpec((rows, width), lambda i, place: (0, 0)),
            scratch_shapes=[
                pltpu.VMEM((rows, 1), F32),
                pltpu.VMEM((rows, 1), F32),
                pltpu.VMEM((rows, width), F32),
            ],
        ),
    )(row_first.reshape(1), query_rows, gathered)


def on_device(queries, keys, values, feat_q, feat_k, samples):
    tok_rows, head_count, head_width = queries.shape
    stretch_count = lax.axis_size("seq")
    both = jnp.concatenate([keys[:, 0], values[:, 0]], axis=1)
    gathered = lax.all_gather(both, "seq", axis=0, tiled=True)
    key_rows = keys[:, 0]
    value_rows = values[:, 0]
    phi_q = features(jnp.einsum("lhd,hdf->hlf", queries, feat_q, preferred_element_type=F32))
    phi_k = features(jnp.einsum("ld,hdf->hlf", key_rows, feat_k, preferred_element_type=F32))
    state = jnp.einsum("hlf,ld->hfd", phi_k, value_rows, preferred_element_type=F32)
    total = jnp.sum(phi_k, axis=1, dtype=F32)
    enter_state, enter_total = prefix_states(state, total)
    causal = jnp.arange(tok_rows)[:, None] >= jnp.arange(tok_rows)[None, :]
    kernel = jnp.einsum("hif,hjf->hij", phi_q, phi_k, preferred_element_type=F32)
    kernel = jnp.where(causal[None], kernel, 0.0)
    numer = jnp.einsum("hij,jd->hid", kernel.astype(jnp.bfloat16), value_rows, preferred_element_type=F32)
    numer = numer + jnp.einsum("hif,hfd->hid", phi_q, enter_state, preferred_element_type=F32)
    denom = jnp.sum(kernel, axis=2) + jnp.sum(phi_q.astype(F32) * enter_total.astype(F32)[:, None, :], axis=2)
    student = jnp.transpose((numer / denom[..., None]).astype(jnp.bfloat16), (1, 0, 2))
    device_index = lax.axis_index("seq")
    picked = samples[device_index]
    row_first = device_index * tok_rows + picked * BLOCK
    query_rows = lax.dynamic_slice_in_dim(queries, picked * BLOCK, BLOCK, 0)
    query_stack = jnp.transpose(query_rows, (1, 0, 2)).reshape(head_count * BLOCK, head_width)
    mixed = teach(row_first, query_stack, gathered).reshape(head_count, BLOCK, head_width)
    teacher = jnp.transpose(mixed, (1, 0, 2))
    student_rows = lax.dynamic_slice_in_dim(student, picked * BLOCK, BLOCK, 0).astype(F32)
    gap = student_rows - teacher
    group = stretch_count * lax.axis_size("head")
    entry_count = group * BLOCK * QH_DEV * HD
    mine = jnp.sum(gap * gap)
    shared = lax.all_to_all(jnp.broadcast_to(mine, (group, 1, 128)), ("seq", "head"), 0, 0)
    loss = jnp.sum(shared[:, 0, 0]) / entry_count
    return (student, teacher[None], loss)


def solution(mesh):
    in_specs = (
        P("seq", "head", None),
        P("seq", "head", None),
        P("seq", "head", None),
        P("head", None, None),
        P("head", None, None),
        P(),
    )
    out_specs = (P("seq", "head", None), P("seq", None, "head", None), P())
    return jax.shard_map(
        on_device, mesh=mesh, in_specs=in_specs, out_specs=out_specs, check_vma=False
    )
```

```python
import functools

import jax
import jax.numpy as jnp
from jax import lax
from jax.experimental import pallas as pl
from jax.experimental.pallas import tpu as pltpu
from jax.sharding import Mesh, PartitionSpec as P

HD = 128
FEAT = 128
QH_DEV = 4
BLOCK = 128
TOK = 256
ROWS = QH_DEV * BLOCK
NY = 4
NZ = 8
MASKED = -1e30
COST = 10000
OWN_COST = 10000
F32 = jnp.float32
BF16 = jnp.bfloat16
LOG2E = 1.4426950408889634
SCORE_SCALE = LOG2E / HD**0.5


def dot_nn(a, b):
    return lax.dot_general(a, b, (((1,), (0,)), ((), ())), preferred_element_type=F32)


def dot_nt(a, b):
    return lax.dot_general(a, b, (((1,), (1,)), ((), ())), preferred_element_type=F32)


def dot_tn(a, b):
    return lax.dot_general(a, b, (((0,), (0,)), ((), ())), preferred_element_type=F32)


def both_softmax(logits, axis):
    scaled = logits * LOG2E
    up = jnp.exp2(scaled - jnp.max(scaled, axis=axis, keepdims=True))
    down = jnp.exp2(jnp.min(scaled, axis=axis, keepdims=True) - scaled)
    up = up * (1.0 / jnp.sum(up, axis=axis, keepdims=True))
    down = down * (1.0 / jnp.sum(down, axis=axis, keepdims=True))
    return jnp.concatenate([up, down], axis=axis).astype(BF16)


def position():
    return lax.axis_index("y"), lax.axis_index("z")


def own_kernel(samples_ref, q_ref, pair_ref, fq_ref, fkt_ref,
               phi_ref, numer_ref, denom_ref, rows_ref, best_ref, total_ref, accum_ref):
    y, z = position()
    picked = samples_ref[y * NZ + z]
    keys = pair_ref[:, :HD]
    vals = pair_ref[:, HD:]
    causal = lax.broadcasted_iota(jnp.int32, (TOK, TOK), 0) >= lax.broadcasted_iota(
        jnp.int32, (TOK, TOK), 1
    )
    for h in range(QH_DEV):
        rows = pl.ds(h * TOK, TOK)
        phi_q = both_softmax(dot_nn(q_ref[h], fq_ref[h]), 1)
        phi_k = both_softmax(dot_nt(fkt_ref[h], keys), 0)
        kernel = jnp.where(causal, dot_nn(phi_q, phi_k), 0.0)
        phi_ref[rows, :] = phi_q
        numer_ref[rows, :] = dot_nn(kernel.astype(BF16), vals)
        denom_ref[rows, :] = jnp.broadcast_to(jnp.sum(kernel, axis=1, keepdims=True), (TOK, HD))
        rows_ref[pl.ds(h * BLOCK, BLOCK), :] = q_ref[h, pl.ds(pl.multiple_of(picked * BLOCK, BLOCK), BLOCK), :]
    scores = dot_nt(keys, rows_ref[...]) * SCORE_SCALE
    place = picked * BLOCK + lax.rem(lax.broadcasted_iota(jnp.int32, scores.shape, 1), BLOCK)
    live = lax.broadcasted_iota(jnp.int32, scores.shape, 0) <= place
    scores = jnp.where(live, scores, MASKED)
    best = jnp.max(scores, axis=0, keepdims=True)
    weights = jnp.exp2(scores - best)
    best_ref[...] = best
    total_ref[...] = jnp.sum(weights, axis=0, keepdims=True)
    accum_ref[...] = dot_tn(vals, weights.astype(BF16))


def own_part(samples, q, pair, fq, fkt):
    vmem = pl.BlockSpec(memory_space=pltpu.VMEM)
    return pl.pallas_call(
        own_kernel,
        out_shape=(
            jax.ShapeDtypeStruct((QH_DEV * TOK, 2 * FEAT), BF16),
            jax.ShapeDtypeStruct((QH_DEV * TOK, HD), F32),
            jax.ShapeDtypeStruct((QH_DEV * TOK, HD), F32),
            jax.ShapeDtypeStruct((ROWS, HD), BF16),
            jax.ShapeDtypeStruct((1, ROWS), F32),
            jax.ShapeDtypeStruct((1, ROWS), F32),
            jax.ShapeDtypeStruct((HD, ROWS), F32),
        ),
        in_specs=[pl.BlockSpec(memory_space=pltpu.SMEM)] + [vmem] * 4,
        out_specs=(vmem,) * 7,
        cost_estimate=pl.CostEstimate(flops=OWN_COST * 10**6, transcendentals=10**6, bytes_accessed=2**21),
    )(samples, q, pair, fq, fkt)


def absorb_kernel(fkt_ref, rows_ref, *refs, where, parts, fresh):
    carried = 3 if fresh else 4
    old, refs = refs[:carried], refs[carried:]
    pieces, refs = refs[:parts], refs[parts:]
    best_ref, total_ref, accum_ref, state_ref, buffer = refs
    y, z = position()
    mine = y * NZ + z
    best_ref[...] = old[0][...]
    total_ref[...] = old[1][...]
    accum_ref[...] = old[2][...]
    state_ref[...] = jnp.zeros(state_ref.shape, F32) if fresh else old[3][...]
    first = 0
    for piece in pieces:
        buffer[pl.ds(first, piece.shape[0]), :] = piece[...]
        first += piece.shape[0]
    ones = jnp.ones((TOK, HD), BF16)

    def one(i, _):
        @pl.when(where(i, y, z) < mine)
        def _():
            span = pl.ds(pl.multiple_of(i * TOK, TOK), TOK)
            keys = buffer[span, :HD]
            vals = buffer[span, HD:]
            scores = dot_nt(keys, rows_ref[...]) * SCORE_SCALE
            best = best_ref[...]
            newtop = jnp.maximum(best, jnp.max(scores, axis=0, keepdims=True))
            fade = jnp.exp2(best - newtop)
            weights = jnp.exp2(scores - newtop)
            best_ref[...] = newtop
            total_ref[...] = fade * total_ref[...] + jnp.sum(weights, axis=0, keepdims=True)
            accum_ref[...] = fade * accum_ref[...] + dot_tn(vals, weights.astype(BF16))
            wide = jnp.concatenate([vals, ones], axis=1)
            for h in range(QH_DEV):
                phi_k = both_softmax(dot_nt(fkt_ref[h], keys), 0)
                rows = pl.ds(h * 2 * FEAT, 2 * FEAT)
                state_ref[rows, :] = state_ref[rows, :] + dot_nn(phi_k, wide)

        return 0

    lax.fori_loop(0, first // TOK, one, 0)


def absorb(fkt, rows, carry, pieces, where):
    vmem = pl.BlockSpec(memory_space=pltpu.VMEM)
    fresh = len(carry) == 3
    return pl.pallas_call(
        functools.partial(absorb_kernel, where=where, parts=len(pieces), fresh=fresh),
        out_shape=(
            jax.ShapeDtypeStruct((1, ROWS), F32),
            jax.ShapeDtypeStruct((1, ROWS), F32),
            jax.ShapeDtypeStruct((HD, ROWS), F32),
            jax.ShapeDtypeStruct((QH_DEV * 2 * FEAT, 2 * HD), F32),
        ),
        in_specs=[vmem] * (2 + len(carry) + len(pieces)),
        out_specs=(vmem,) * 4,
        scratch_shapes=[pltpu.VMEM((sum(p.shape[0] for p in pieces), 2 * HD), BF16)],
        cost_estimate=pl.CostEstimate(flops=COST * 10**6, transcendentals=10**6, bytes_accessed=2**21),
    )(fkt, rows, *carry, *pieces)


def last_kernel(samples_ref, phi_ref, numer_ref, denom_ref, best_ref, total_ref, accum_ref, state_ref,
                student_ref, teacher_ref, square_ref, keep):
    y, z = position()
    picked = samples_ref[y * NZ + z]
    for h in range(QH_DEV):
        rows = pl.ds(h * TOK, TOK)
        state = state_ref[pl.ds(h * 2 * FEAT, 2 * FEAT), :].astype(BF16)
        across = dot_nn(phi_ref[rows, :], state)
        ratio = (numer_ref[rows, :] + across[:, :HD]) / (denom_ref[rows, :] + across[:, HD:])
        ratio = ratio.astype(BF16)
        student_ref[h] = ratio
        keep[h] = ratio.astype(F32)
    mixed = jnp.transpose(accum_ref[...] / total_ref[...])
    squares = jnp.zeros((BLOCK, HD), F32)
    for h in range(QH_DEV):
        teacher = mixed[h * BLOCK:(h + 1) * BLOCK]
        teacher_ref[h] = teacher
        gap = keep[h, pl.ds(pl.multiple_of(picked * BLOCK, BLOCK), BLOCK), :] - teacher
        squares = squares + gap * gap
    square_ref[...] = jnp.full(square_ref.shape, jnp.sum(squares), F32)


def last_part(samples, phi, numer, denom, carry, group):
    vmem = pl.BlockSpec(memory_space=pltpu.VMEM)
    return pl.pallas_call(
        last_kernel,
        out_shape=(
            jax.ShapeDtypeStruct((QH_DEV, TOK, HD), BF16),
            jax.ShapeDtypeStruct((QH_DEV, BLOCK, HD), F32),
            jax.ShapeDtypeStruct((group, 1, 128), F32),
        ),
        in_specs=[pl.BlockSpec(memory_space=pltpu.SMEM)] + [vmem] * 7,
        out_specs=(vmem,) * 3,
        scratch_shapes=[pltpu.VMEM((QH_DEV, TOK, HD), F32)],
    )(samples, phi, numer, denom, *carry)


def along_z(x, step):
    return lax.ppermute(x, "z", [(z, (z + step) % NZ) for z in range(NZ)])


def on_device(queries, keys, values, feat_q, feat_k, samples):
    group = lax.axis_size("y") * lax.axis_size("z") * lax.axis_size("head")
    pair = jnp.concatenate([keys[:, 0], values[:, 0]], axis=1)
    column = lax.all_to_all(jnp.broadcast_to(pair[None], (NY,) + pair.shape), "y", 0, 0)
    column = column.reshape(NY * TOK, 2 * HD)
    q = jnp.transpose(queries, (1, 0, 2))
    fkt = jnp.transpose(feat_k, (0, 2, 1))
    phi, numer, denom, rows, *carry = own_part(samples, q, pair, feat_q, fkt)
    up = down = column
    carry = absorb(fkt, rows, carry, [column], lambda i, y, z: i * NZ + z + jnp.where(i == y, NZ * NY, 0))
    half = column.shape[0] // 2
    for k in range(1, 4):
        up, down = along_z(up, 1), along_z(down, -1)
        carry = absorb(
            fkt, rows, carry, [up, down],
            lambda i, y, z, k=k: lax.rem(i, NY) * NZ
            + lax.rem(z + jnp.where(i < NY, NZ - k, k), NZ),
        )
    up, down = along_z(up[:half], 1), along_z(down[half:], -1)
    carry = absorb(fkt, rows, carry, [up, down], lambda i, y, z: i * NZ + lax.rem(z + 4, NZ))
    student, teacher, square = last_part(samples, phi, numer, denom, carry, group)
    shared = lax.all_to_all(square, ("y", "z", "head"), 0, 0)
    loss = jnp.sum(shared[:, 0, 0]) / (group * BLOCK * QH_DEV * HD)
    return (
        jnp.transpose(student, (1, 0, 2)),
        jnp.transpose(teacher, (1, 0, 2))[None],
        loss,
    )


def solution(mesh):
    head = mesh.shape["head"]
    torus = Mesh(mesh.devices.reshape(NY, NZ, head), ("y", "z", "head"))
    seq = ("y", "z")
    in_specs = (
        P(seq, "head", None),
        P(seq, "head", None),
        P(seq, "head", None),
        P("head", None, None),
        P("head", None, None),
        P(),
    )
    out_specs = (P(seq, "head", None), P(seq, None, "head", None), P())
    return jax.shard_map(
        on_device, mesh=torus, in_specs=in_specs, out_specs=out_specs, check_vma=False
    )
```

```python
import functools

import jax
import jax.numpy as jnp
from jax import lax
from jax.experimental import pallas as pl
from jax.experimental.pallas import tpu as pltpu
from jax.sharding import Mesh, PartitionSpec as P

HD = 128
FEAT = 128
QH_DEV = 4
BLOCK = 128
TOK = 256
ROWS = QH_DEV * BLOCK
NY = 4
NZ = 8
MASKED = -1e30
COST = 10000
OWN_COST = 10000
F32 = jnp.float32
BF16 = jnp.bfloat16
LOG2E = 1.4426950408889634
SCORE_SCALE = LOG2E / HD**0.5


def dot_nn(a, b):
    return lax.dot_general(a, b, (((1,), (0,)), ((), ())), preferred_element_type=F32)


def dot_nt(a, b):
    return lax.dot_general(a, b, (((1,), (1,)), ((), ())), preferred_element_type=F32)


def dot_tn(a, b):
    return lax.dot_general(a, b, (((0,), (0,)), ((), ())), preferred_element_type=F32)


def both_softmax(logits, axis):
    scaled = logits * LOG2E
    up = jnp.exp2(scaled - jnp.max(scaled, axis=axis, keepdims=True))
    down = jnp.exp2(jnp.min(scaled, axis=axis, keepdims=True) - scaled)
    up = up * (1.0 / jnp.sum(up, axis=axis, keepdims=True))
    down = down * (1.0 / jnp.sum(down, axis=axis, keepdims=True))
    return jnp.concatenate([up, down], axis=axis).astype(BF16)


def position():
    return lax.axis_index("y"), lax.axis_index("z")


def own_kernel(samples_ref, q_ref, pair_ref, fq_ref, fkt_ref,
               phi_ref, numer_ref, denom_ref, rows_ref, best_ref, total_ref, accum_ref):
    y, z = position()
    picked = samples_ref[y * NZ + z]
    keys = pair_ref[:, :HD]
    vals = pair_ref[:, HD:]
    causal = lax.broadcasted_iota(jnp.int32, (TOK, TOK), 0) >= lax.broadcasted_iota(
        jnp.int32, (TOK, TOK), 1
    )
    for h in range(QH_DEV):
        rows = pl.ds(h * TOK, TOK)
        phi_q = both_softmax(dot_nn(q_ref[h], fq_ref[h]), 1)
        phi_k = both_softmax(dot_nt(fkt_ref[h], keys), 0)
        kernel = jnp.where(causal, dot_nn(phi_q, phi_k), 0.0)
        phi_ref[rows, :] = phi_q
        numer_ref[rows, :] = dot_nn(kernel.astype(BF16), vals)
        denom_ref[rows, :] = jnp.broadcast_to(jnp.sum(kernel, axis=1, keepdims=True), (TOK, HD))
        rows_ref[pl.ds(h * BLOCK, BLOCK), :] = q_ref[h, pl.ds(pl.multiple_of(picked * BLOCK, BLOCK), BLOCK), :]
    scores = dot_nt(keys, rows_ref[...]) * SCORE_SCALE
    place = picked * BLOCK + lax.rem(lax.broadcasted_iota(jnp.int32, scores.shape, 1), BLOCK)
    live = lax.broadcasted_iota(jnp.int32, scores.shape, 0) <= place
    scores = jnp.where(live, scores, MASKED)
    best = jnp.max(scores, axis=0, keepdims=True)
    weights = jnp.exp2(scores - best)
    best_ref[...] = best
    total_ref[...] = jnp.sum(weights, axis=0, keepdims=True)
    accum_ref[...] = dot_tn(vals, weights.astype(BF16))


def own_part(samples, q, pair, fq, fkt):
    vmem = pl.BlockSpec(memory_space=pltpu.VMEM)
    return pl.pallas_call(
        own_kernel,
        out_shape=(
            jax.ShapeDtypeStruct((QH_DEV * TOK, 2 * FEAT), BF16),
            jax.ShapeDtypeStruct((QH_DEV * TOK, HD), F32),
            jax.ShapeDtypeStruct((QH_DEV * TOK, HD), F32),
            jax.ShapeDtypeStruct((ROWS, HD), BF16),
            jax.ShapeDtypeStruct((1, ROWS), F32),
            jax.ShapeDtypeStruct((1, ROWS), F32),
            jax.ShapeDtypeStruct((HD, ROWS), F32),
        ),
        in_specs=[pl.BlockSpec(memory_space=pltpu.SMEM)] + [vmem] * 4,
        out_specs=(vmem,) * 7,
        cost_estimate=pl.CostEstimate(flops=OWN_COST * 10**6, transcendentals=10**6, bytes_accessed=2**21),
    )(samples, q, pair, fq, fkt)


def take_in(fkt_ref, rows_ref, old, pieces, best_ref, total_ref, accum_ref, state_ref,
            buffer, first_ref, second_ref, scores_ref, weights_ref, phi_ref, where):
    y, z = position()
    mine = y * NZ + z
    blocks = buffer.shape[0] // TOK
    live = [where(i, y, z) < mine for i in range(blocks)]
    some = functools.reduce(jnp.logical_or, live)
    if old[3] is None:
        state_ref[...] = jnp.zeros(state_ref.shape, F32)
    else:
        state_ref[...] = old[3][...]

    @pl.when(jnp.logical_not(some))
    def _():
        best_ref[...] = old[0][...]
        total_ref[...] = old[1][...]
        accum_ref[...] = old[2][...]

    @pl.when(some)
    def _():
        begin = 0
        for piece in pieces:
            buffer[pl.ds(begin, piece.shape[0]), :] = piece[...]
            begin += piece.shape[0]

        def span(i):
            return pl.ds(pl.multiple_of(i * TOK, TOK), TOK)

        def logits(i, to):
            keys = buffer[span(i), :HD]
            for h in range(QH_DEV):
                to[h] = dot_nt(fkt_ref[h], keys)

        def score(i, top):
            scores = dot_nt(buffer[span(i), :HD], rows_ref[...])
            scores_ref[span(i), :] = scores
            peak = jnp.max(scores.reshape(TOK // 8, 8, ROWS), axis=0)
            return jnp.maximum(top, jnp.where(where(i, y, z) < mine, peak, MASKED))

        def feature(i, out_of):
            keep = jnp.where(where(i, y, z) < mine, 1.0, 0.0).astype(F32)
            for h in range(QH_DEV):
                for half in range(2):
                    part = out_of[h, :, half * 128:(half + 1) * 128] * LOG2E
                    up = jnp.exp2(part - jnp.max(part, axis=0, keepdims=True))
                    down = jnp.exp2(jnp.min(part, axis=0, keepdims=True) - part)
                    up = up * (keep / jnp.sum(up, axis=0, keepdims=True))
                    down = down * (keep / jnp.sum(down, axis=0, keepdims=True))
                    to = pl.ds(pl.multiple_of(i * TOK, TOK) + half * 128, 128)
                    phi_ref[pl.ds(h * 2 * FEAT, FEAT), to] = up.astype(BF16)
                    phi_ref[pl.ds(h * 2 * FEAT + FEAT, FEAT), to] = down.astype(BF16)

        logits(0, first_ref)

        def two(j, top):
            i = 2 * j
            logits(i + 1, second_ref)
            feature(i, first_ref)
            top = score(i, top)
            logits(jnp.minimum(i + 2, blocks - 1), first_ref)
            feature(i + 1, second_ref)
            return score(i + 1, top)

        top = lax.fori_loop(0, blocks // 2, two, jnp.full((8, ROWS), MASKED, F32))
        best = old[0][...]
        newtop = jnp.maximum(best, jnp.max(top, axis=0, keepdims=True) * SCORE_SCALE)
        fade = jnp.exp2(best - newtop)
        best_ref[...] = newtop
        sums = jnp.zeros((8, ROWS), F32)
        ones = jnp.ones((blocks * TOK, HD), BF16)
        wide = jnp.concatenate([buffer[:, HD:], ones], axis=1)
        state_ref[...] = state_ref[...] + dot_nn(phi_ref[...], wide)
        for i in range(blocks):
            shift = jnp.where(live[i], newtop, -MASKED)
            weights = jnp.exp2(scores_ref[pl.ds(i * TOK, TOK), :] * SCORE_SCALE - shift)
            sums = sums + jnp.sum(weights.reshape(TOK // 8, 8, ROWS), axis=0)
            weights_ref[pl.ds(i * TOK, TOK), :] = weights.astype(BF16)
        total_ref[...] = fade * old[1][...] + jnp.sum(sums, axis=0, keepdims=True)
        accum_ref[...] = fade * old[2][...] + dot_tn(buffer[:, HD:], weights_ref[...])


def work_space(blocks):
    return [
        pltpu.VMEM((blocks * TOK, 2 * HD), BF16),
        pltpu.VMEM((QH_DEV, FEAT, TOK), F32),
        pltpu.VMEM((QH_DEV, FEAT, TOK), F32),
        pltpu.VMEM((blocks * TOK, ROWS), F32),
        pltpu.VMEM((blocks * TOK, ROWS), BF16),
        pltpu.VMEM((QH_DEV * 2 * FEAT, blocks * TOK), BF16),
    ]


CARRY = (
    jax.ShapeDtypeStruct((1, ROWS), F32),
    jax.ShapeDtypeStruct((1, ROWS), F32),
    jax.ShapeDtypeStruct((HD, ROWS), F32),
    jax.ShapeDtypeStruct((QH_DEV * 2 * FEAT, 2 * HD), F32),
)


def absorb_kernel(fkt_ref, rows_ref, *refs, where, parts, fresh):
    carried = 3 if fresh else 4
    old = refs[:3] + ((None,) if fresh else (refs[3],))
    pieces = refs[carried:carried + parts]
    take_in(fkt_ref, rows_ref, old, pieces, *refs[carried + parts:], where)


def absorb(fkt, rows, carry, pieces, where):
    vmem = pl.BlockSpec(memory_space=pltpu.VMEM)
    fresh = len(carry) == 3
    return pl.pallas_call(
        functools.partial(absorb_kernel, where=where, parts=len(pieces), fresh=fresh),
        out_shape=CARRY,
        in_specs=[vmem] * (2 + len(carry) + len(pieces)),
        out_specs=(vmem,) * 4,
        scratch_shapes=work_space(sum(p.shape[0] for p in pieces) // TOK),
        cost_estimate=pl.CostEstimate(flops=COST * 10**6, transcendentals=10**6, bytes_accessed=2**21),
    )(fkt, rows, *carry, *pieces)


def last_kernel(samples_ref, fkt_ref, rows_ref, *refs, where, parts):
    old, pieces, refs = refs[:4], refs[4:4 + parts], refs[4 + parts:]
    phi_ref, numer_ref, denom_ref, student_ref, teacher_ref, square_ref, keep = refs[:7]
    carry = refs[7:11]
    take_in(fkt_ref, rows_ref, old, pieces, *refs[7:], where)
    total_ref, accum_ref, state_ref = carry[1:]
    y, z = position()
    picked = samples_ref[y * NZ + z]
    for h in range(QH_DEV):
        rows = pl.ds(h * TOK, TOK)
        state = state_ref[pl.ds(h * 2 * FEAT, 2 * FEAT), :].astype(BF16)
        across = dot_nn(phi_ref[rows, :], state)
        ratio = (numer_ref[rows, :] + across[:, :HD]) / (denom_ref[rows, :] + across[:, HD:])
        ratio = ratio.astype(BF16)
        student_ref[h] = ratio
        keep[h] = ratio.astype(F32)
    mixed = jnp.transpose(accum_ref[...] / total_ref[...])
    squares = jnp.zeros((BLOCK, HD), F32)
    for h in range(QH_DEV):
        teacher = mixed[h * BLOCK:(h + 1) * BLOCK]
        teacher_ref[h] = teacher
        gap = keep[h, pl.ds(pl.multiple_of(picked * BLOCK, BLOCK), BLOCK), :] - teacher
        squares = squares + gap * gap
    square_ref[...] = jnp.full(square_ref.shape, jnp.sum(squares), F32)


def last_part(samples, fkt, rows, carry, pieces, where, phi, numer, denom, group):
    vmem = pl.BlockSpec(memory_space=pltpu.VMEM)
    return pl.pallas_call(
        functools.partial(last_kernel, where=where, parts=len(pieces)),
        out_shape=(
            jax.ShapeDtypeStruct((QH_DEV, TOK, HD), BF16),
            jax.ShapeDtypeStruct((QH_DEV, BLOCK, HD), F32),
            jax.ShapeDtypeStruct((group, 1, 128), F32),
        ),
        in_specs=[pl.BlockSpec(memory_space=pltpu.SMEM)] + [vmem] * (9 + len(pieces)),
        out_specs=(vmem,) * 3,
        scratch_shapes=[pltpu.VMEM((QH_DEV, TOK, HD), F32)]
        + [pltpu.VMEM(c.shape, c.dtype) for c in CARRY]
        + work_space(sum(p.shape[0] for p in pieces) // TOK),
    )(samples, fkt, rows, *carry, *pieces, phi, numer, denom)


def along_z(x, step):
    return lax.ppermute(x, "z", [(z, (z + step) % NZ) for z in range(NZ)])


def on_device(queries, keys, values, feat_q, feat_k, samples):
    group = lax.axis_size("y") * lax.axis_size("z") * lax.axis_size("head")
    pair = jnp.concatenate([keys[:, 0], values[:, 0]], axis=1)
    column = lax.all_to_all(jnp.broadcast_to(pair[None], (NY,) + pair.shape), "y", 0, 0)
    column = column.reshape(NY * TOK, 2 * HD)
    q = jnp.transpose(queries, (1, 0, 2))
    fkt = jnp.transpose(feat_k, (0, 2, 1))
    phi, numer, denom, rows, *carry = own_part(samples, q, pair, feat_q, fkt)
    up = down = column
    carry = absorb(fkt, rows, carry, [column], lambda i, y, z: i * NZ + z + jnp.where(i == y, NZ * NY, 0))
    half = column.shape[0] // 2
    for k in range(1, 4):
        up, down = along_z(up, 1), along_z(down, -1)
        carry = absorb(
            fkt, rows, carry, [up, down],
            lambda i, y, z, k=k: lax.rem(i, NY) * NZ
            + lax.rem(z + jnp.where(i < NY, NZ - k, k), NZ),
        )
    up, down = along_z(up[:half], 1), along_z(down[half:], -1)
    student, teacher, square = last_part(
        samples, fkt, rows, carry, [up, down], lambda i, y, z: i * NZ + lax.rem(z + 4, NZ),
        phi, numer, denom, group,
    )
    shared = lax.all_to_all(square, ("y", "z", "head"), 0, 0)
    loss = jnp.sum(shared[:, 0, 0]) / (group * BLOCK * QH_DEV * HD)
    return (
        jnp.transpose(student, (1, 0, 2)),
        jnp.transpose(teacher, (1, 0, 2))[None],
        loss,
    )


def solution(mesh):
    head = mesh.shape["head"]
    torus = Mesh(mesh.devices.reshape(NY, NZ, head), ("y", "z", "head"))
    seq = ("y", "z")
    in_specs = (
        P(seq, "head", None),
        P(seq, "head", None),
        P(seq, "head", None),
        P("head", None, None),
        P("head", None, None),
        P(),
    )
    out_specs = (P(seq, "head", None), P(seq, None, "head", None), P())
    return jax.shard_map(
        on_device, mesh=torus, in_specs=in_specs, out_specs=out_specs, check_vma=False
    )
```

```python
import functools

import jax
import jax.numpy as jnp
from jax import lax
from jax.experimental import pallas as pl
from jax.experimental.pallas import tpu as pltpu
from jax.sharding import Mesh, PartitionSpec as P

HD = 128
FEAT = 128
QH_DEV = 4
BLOCK = 128
TOK = 256
ROWS = QH_DEV * BLOCK
NY = 4
NZ = 8
MASKED = -1e30
COST = 10000
OWN_VMEM = 12 * 2**20
VMEM = 28 * 2**20
OWN_COST = 10000
F32 = jnp.float32
BF16 = jnp.bfloat16
LOG2E = 1.4426950408889634
SCORE_SCALE = LOG2E / HD**0.5


def dot_nn(a, b):
    return lax.dot_general(a, b, (((1,), (0,)), ((), ())), preferred_element_type=F32)


def dot_nt(a, b):
    return lax.dot_general(a, b, (((1,), (1,)), ((), ())), preferred_element_type=F32)


def dot_tn(a, b):
    return lax.dot_general(a, b, (((0,), (0,)), ((), ())), preferred_element_type=F32)


def both_softmax(logits, axis):
    up = jnp.exp(logits - jnp.max(logits, axis=axis, keepdims=True))
    down = jnp.exp(jnp.min(logits, axis=axis, keepdims=True) - logits)
    up = up * (1.0 / jnp.sum(up, axis=axis, keepdims=True))
    down = down * (1.0 / jnp.sum(down, axis=axis, keepdims=True))
    return jnp.concatenate([up, down], axis=axis).astype(BF16)


def position():
    return lax.axis_index("y"), lax.axis_index("z")


def own_kernel(samples_ref, q_ref, k_ref, v_ref, fq_ref, fkt_ref,
               phi_ref, numer_ref, denom_ref, rows_ref, best_ref, total_ref, accum_ref):
    y, z = position()
    picked = samples_ref[y * NZ + z]
    keys = k_ref[...]
    vals = v_ref[...]
    causal = lax.broadcasted_iota(jnp.int32, (TOK, TOK), 0) >= lax.broadcasted_iota(
        jnp.int32, (TOK, TOK), 1
    )
    for h in range(QH_DEV):
        rows = pl.ds(h * TOK, TOK)
        phi_q = both_softmax(dot_nn(q_ref[h], fq_ref[h]), 1)
        phi_k = both_softmax(dot_nt(fkt_ref[h], keys), 0)
        kernel = jnp.where(causal, dot_nn(phi_q, phi_k), 0.0)
        phi_ref[rows, :] = phi_q
        numer_ref[rows, :] = dot_nn(kernel.astype(BF16), vals)
        denom_ref[rows, :] = jnp.broadcast_to(jnp.sum(kernel, axis=1, keepdims=True), (TOK, HD))
        rows_ref[pl.ds(h * BLOCK, BLOCK), :] = q_ref[h, pl.ds(pl.multiple_of(picked * BLOCK, BLOCK), BLOCK), :]
    scores = dot_nt(keys, rows_ref[...]) * SCORE_SCALE
    place = picked * BLOCK + lax.rem(lax.broadcasted_iota(jnp.int32, scores.shape, 1), BLOCK)
    live = lax.broadcasted_iota(jnp.int32, scores.shape, 0) <= place
    scores = jnp.where(live, scores, MASKED)
    best = jnp.max(scores, axis=0, keepdims=True)
    weights = jnp.exp2(scores - best)
    best_ref[...] = best
    total_ref[...] = jnp.sum(weights, axis=0, keepdims=True)
    accum_ref[...] = dot_tn(vals, weights.astype(BF16))


def own_part(samples, q, k, v, fq, fkt):
    vmem = pl.BlockSpec(memory_space=pltpu.VMEM)
    return pl.pallas_call(
        own_kernel,
        out_shape=(
            jax.ShapeDtypeStruct((QH_DEV * TOK, 2 * FEAT), BF16),
            jax.ShapeDtypeStruct((QH_DEV * TOK, HD), F32),
            jax.ShapeDtypeStruct((QH_DEV * TOK, HD), F32),
            jax.ShapeDtypeStruct((ROWS, HD), BF16),
            jax.ShapeDtypeStruct((1, ROWS), F32),
            jax.ShapeDtypeStruct((1, ROWS), F32),
            jax.ShapeDtypeStruct((HD, ROWS), F32),
        ),
        in_specs=[pl.BlockSpec(memory_space=pltpu.SMEM)] + [vmem] * 5,
        out_specs=(vmem,) * 7,
        compiler_params=pltpu.CompilerParams(vmem_limit_bytes=OWN_VMEM),
        cost_estimate=pl.CostEstimate(flops=OWN_COST * 10**6, transcendentals=10**6, bytes_accessed=2**21),
    )(samples, q, k, v, fq, fkt)


def take_in(fkt_ref, rows_ref, old, pieces, best_ref, total_ref, accum_ref, state_ref,
            first_ref, second_ref, scores_ref, where):
    y, z = position()
    mine = y * NZ + z
    blocks = scores_ref.shape[0] // TOK
    live = [where(i, y, z) < mine for i in range(blocks)]
    some = functools.reduce(jnp.logical_or, live)
    if old[3] is None:
        state_ref[...] = jnp.zeros(state_ref.shape, F32)
    else:
        state_ref[...] = old[3][...]

    @pl.when(jnp.logical_not(some))
    def _():
        best_ref[...] = old[0][...]
        total_ref[...] = old[1][...]
        accum_ref[...] = old[2][...]

    def go(buffer, weights_ref, phi_ref):
        begin = 0
        for piece in pieces:
            buffer[pl.ds(begin, piece.shape[0]), :] = piece[...]
            begin += piece.shape[0]

        def span(i):
            return pl.ds(pl.multiple_of(i * TOK, TOK), TOK)

        def logits(i, to):
            keys = buffer[span(i), :HD]
            for h in range(QH_DEV):
                to[h] = dot_nt(fkt_ref[h], keys)

        def score(i, top):
            scores = dot_nt(buffer[span(i), :HD], rows_ref[...])
            scores_ref[span(i), :] = scores
            peak = jnp.max(scores.reshape(TOK // 8, 8, ROWS), axis=0)
            return jnp.maximum(top, jnp.where(where(i, y, z) < mine, peak, MASKED))

        def feature(i, out_of):
            keep = jnp.where(where(i, y, z) < mine, 1.0, 0.0).astype(F32)
            for h in range(QH_DEV):
                for half in range(2):
                    part = out_of[h, :, half * 128:(half + 1) * 128]
                    up = jnp.exp(part - jnp.max(part, axis=0, keepdims=True))
                    down = jnp.exp(jnp.min(part, axis=0, keepdims=True) - part)
                    up = up * (keep / jnp.sum(up, axis=0, keepdims=True))
                    down = down * (keep / jnp.sum(down, axis=0, keepdims=True))
                    to = pl.ds(pl.multiple_of(i * TOK, TOK) + half * 128, 128)
                    phi_ref[pl.ds(h * 2 * FEAT, FEAT), to] = up.astype(BF16)
                    phi_ref[pl.ds(h * 2 * FEAT + FEAT, FEAT), to] = down.astype(BF16)

        logits(0, first_ref)

        def two(j, top):
            i = 2 * j
            logits(i + 1, second_ref)
            feature(i, first_ref)
            top = score(i, top)
            logits(jnp.minimum(i + 2, blocks - 1), first_ref)
            feature(i + 1, second_ref)
            return score(i + 1, top)

        top = lax.fori_loop(0, blocks // 2, two, jnp.full((8, ROWS), MASKED, F32))
        best = old[0][...]
        newtop = jnp.maximum(best, jnp.max(top, axis=0, keepdims=True) * SCORE_SCALE)
        fade = jnp.exp2(best - newtop)
        best_ref[...] = newtop
        sums = jnp.zeros((8, ROWS), F32)
        ones = jnp.ones((blocks * TOK, HD), BF16)
        wide = jnp.concatenate([buffer[:, HD:], ones], axis=1)
        state_ref[...] = state_ref[...] + dot_nn(phi_ref[...], wide)
        for i in range(blocks):
            shift = jnp.where(live[i], newtop, -MASKED)
            weights = jnp.exp2(scores_ref[pl.ds(i * TOK, TOK), :] * SCORE_SCALE - shift)
            sums = sums + jnp.sum(weights.reshape(TOK // 8, 8, ROWS), axis=0)
            weights_ref[pl.ds(i * TOK, TOK), :] = weights.astype(BF16)
        total_ref[...] = fade * old[1][...] + jnp.sum(sums, axis=0, keepdims=True)
        accum_ref[...] = fade * old[2][...] + dot_tn(buffer[:, HD:], weights_ref[...])

    @pl.when(some)
    def _():
        pl.run_scoped(
            go,
            pltpu.VMEM((blocks * TOK, 2 * HD), BF16),
            pltpu.VMEM((blocks * TOK, ROWS), BF16),
            pltpu.VMEM((QH_DEV * 2 * FEAT, blocks * TOK), BF16),
        )


def work_space(blocks):
    return [
        pltpu.VMEM((QH_DEV, FEAT, TOK), F32),
        pltpu.VMEM((QH_DEV, FEAT, TOK), F32),
        pltpu.VMEM((blocks * TOK, ROWS), F32),
    ]


CARRY = (
    jax.ShapeDtypeStruct((1, ROWS), F32),
    jax.ShapeDtypeStruct((1, ROWS), F32),
    jax.ShapeDtypeStruct((HD, ROWS), F32),
    jax.ShapeDtypeStruct((QH_DEV * 2 * FEAT, 2 * HD), F32),
)


def absorb_kernel(fkt_ref, rows_ref, *refs, where, parts, fresh):
    carried = 3 if fresh else 4
    old = refs[:3] + ((None,) if fresh else (refs[3],))
    pieces = refs[carried:carried + parts]
    take_in(fkt_ref, rows_ref, old, pieces, *refs[carried + parts:], where)


def absorb(fkt, rows, carry, pieces, where):
    vmem = pl.BlockSpec(memory_space=pltpu.VMEM)
    fresh = len(carry) == 3
    return pl.pallas_call(
        functools.partial(absorb_kernel, where=where, parts=len(pieces), fresh=fresh),
        out_shape=CARRY,
        in_specs=[vmem] * (2 + len(carry) + len(pieces)),
        out_specs=(vmem,) * 4,
        scratch_shapes=work_space(sum(p.shape[0] for p in pieces) // TOK),
        compiler_params=pltpu.CompilerParams(vmem_limit_bytes=VMEM),
        cost_estimate=pl.CostEstimate(flops=COST * 10**6, transcendentals=10**6, bytes_accessed=2**21),
    )(fkt, rows, *carry, *pieces)


def last_kernel(samples_ref, fkt_ref, rows_ref, *refs, where, parts):
    old, pieces, refs = refs[:4], refs[4:4 + parts], refs[4 + parts:]
    phi_ref, numer_ref, denom_ref, student_ref, teacher_ref, square_ref, keep = refs[:7]
    carry = refs[7:11]
    take_in(fkt_ref, rows_ref, old, pieces, *refs[7:], where)
    total_ref, accum_ref, state_ref = carry[1:]
    y, z = position()
    picked = samples_ref[y * NZ + z]
    for h in range(QH_DEV):
        rows = pl.ds(h * TOK, TOK)
        state = state_ref[pl.ds(h * 2 * FEAT, 2 * FEAT), :].astype(BF16)
        across = dot_nn(phi_ref[rows, :], state)
        ratio = (numer_ref[rows, :] + across[:, :HD]) / (denom_ref[rows, :] + across[:, HD:])
        ratio = ratio.astype(BF16)
        student_ref[h] = ratio
        keep[h] = ratio.astype(F32)
    mixed = jnp.transpose(accum_ref[...] / total_ref[...])
    squares = jnp.zeros((BLOCK, HD), F32)
    for h in range(QH_DEV):
        teacher = mixed[h * BLOCK:(h + 1) * BLOCK]
        teacher_ref[h] = teacher
        gap = keep[h, pl.ds(pl.multiple_of(picked * BLOCK, BLOCK), BLOCK), :] - teacher
        squares = squares + gap * gap
    square_ref[...] = jnp.full(square_ref.shape, jnp.sum(squares), F32)


def last_part(samples, fkt, rows, carry, pieces, where, phi, numer, denom, group):
    vmem = pl.BlockSpec(memory_space=pltpu.VMEM)
    return pl.pallas_call(
        functools.partial(last_kernel, where=where, parts=len(pieces)),
        out_shape=(
            jax.ShapeDtypeStruct((QH_DEV, TOK, HD), BF16),
            jax.ShapeDtypeStruct((QH_DEV, BLOCK, HD), F32),
            jax.ShapeDtypeStruct((group, 1, 128), F32),
        ),
        in_specs=[pl.BlockSpec(memory_space=pltpu.SMEM)] + [vmem] * (9 + len(pieces)),
        out_specs=(vmem,) * 3,
        scratch_shapes=[pltpu.VMEM((QH_DEV, TOK, HD), F32)]
        + [pltpu.VMEM(c.shape, c.dtype) for c in CARRY]
        + work_space(sum(p.shape[0] for p in pieces) // TOK),
        compiler_params=pltpu.CompilerParams(vmem_limit_bytes=VMEM),
    )(samples, fkt, rows, *carry, *pieces, phi, numer, denom)


def along_z(x, step):
    return lax.ppermute(x, "z", [(z, (z + step) % NZ) for z in range(NZ)])


def on_device(queries, keys, values, feat_q, feat_k, samples):
    group = lax.axis_size("y") * lax.axis_size("z") * lax.axis_size("head")
    wide = (NY, TOK, HD)
    pair = jnp.concatenate(
        [jnp.broadcast_to(keys[:, 0][None], wide), jnp.broadcast_to(values[:, 0][None], wide)], axis=2
    )
    column = lax.all_to_all(pair, "y", 0, 0)
    column = column.reshape(NY * TOK, 2 * HD)
    q = jnp.transpose(queries, (1, 0, 2))
    fkt = jnp.transpose(feat_k, (0, 2, 1))
    phi, numer, denom, rows, *carry = own_part(samples, q, keys[:, 0], values[:, 0], feat_q, fkt)
    up = down = column
    carry = absorb(fkt, rows, carry, [column], lambda i, y, z: i * NZ + z + jnp.where(i == y, NZ * NY, 0))
    half = column.shape[0] // 2
    for k in range(1, 4):
        up, down = along_z(up, 1), along_z(down, -1)
        carry = absorb(
            fkt, rows, carry, [up, down],
            lambda i, y, z, k=k: lax.rem(i, NY) * NZ
            + lax.rem(z + jnp.where(i < NY, NZ - k, k), NZ),
        )
    up, down = along_z(up[:half], 1), along_z(down[half:], -1)
    student, teacher, square = last_part(
        samples, fkt, rows, carry, [up, down], lambda i, y, z: i * NZ + lax.rem(z + 4, NZ),
        phi, numer, denom, group,
    )
    shared = lax.all_to_all(square, ("y", "z", "head"), 0, 0)
    loss = jnp.sum(shared[:, 0, 0]) / (group * BLOCK * QH_DEV * HD)
    return (
        jnp.transpose(student, (1, 0, 2)),
        jnp.transpose(teacher, (1, 0, 2))[None],
        loss,
    )


def solution(mesh):
    head = mesh.shape["head"]
    torus = Mesh(mesh.devices.reshape(NY, NZ, head), ("y", "z", "head"))
    seq = ("y", "z")
    in_specs = (
        P(seq, "head", None),
        P(seq, "head", None),
        P(seq, "head", None),
        P("head", None, None),
        P("head", None, None),
        P(),
    )
    out_specs = (P(seq, "head", None), P(seq, None, "head", None), P())
    return jax.shard_map(
        on_device, mesh=torus, in_specs=in_specs, out_specs=out_specs, check_vma=False
    )
```

```python
import functools

import jax
import jax.numpy as jnp
from jax import lax
from jax.experimental import pallas as pl
from jax.experimental.pallas import tpu as pltpu
from jax.sharding import Mesh, PartitionSpec as P

HD = 128
FEAT = 128
QH_DEV = 4
BLOCK = 128
TOK = 256
ROWS = QH_DEV * BLOCK
NY = 4
NZ = 8
MASKED = -1e30
COST = 10000
OWN_VMEM = 12 * 2**20
VMEM = 28 * 2**20
OWN_COST = 10000
F32 = jnp.float32
BF16 = jnp.bfloat16
LOG2E = 1.4426950408889634
SCORE_SCALE = LOG2E / HD**0.5


def dot_nn(a, b):
    return lax.dot_general(a, b, (((1,), (0,)), ((), ())), preferred_element_type=F32)


def dot_nt(a, b):
    return lax.dot_general(a, b, (((1,), (1,)), ((), ())), preferred_element_type=F32)


def dot_tn(a, b):
    return lax.dot_general(a, b, (((0,), (0,)), ((), ())), preferred_element_type=F32)


def both_softmax(logits, axis):
    up = jnp.exp(logits - jnp.max(logits, axis=axis, keepdims=True))
    down = jnp.exp(jnp.min(logits, axis=axis, keepdims=True) - logits)
    up = up * (1.0 / jnp.sum(up, axis=axis, keepdims=True))
    down = down * (1.0 / jnp.sum(down, axis=axis, keepdims=True))
    return jnp.concatenate([up, down], axis=axis).astype(BF16)


def position():
    return lax.axis_index("y"), lax.axis_index("z")


def own_kernel(samples_ref, q_ref, k_ref, v_ref, fq_ref, fkt_ref,
               phi_ref, numer_ref, denom_ref, rows_ref, best_ref, total_ref, accum_ref):
    y, z = position()
    picked = samples_ref[y * NZ + z]
    keys = k_ref[...]
    vals = v_ref[...]
    causal = lax.broadcasted_iota(jnp.int32, (TOK, TOK), 0) >= lax.broadcasted_iota(
        jnp.int32, (TOK, TOK), 1
    )
    for h in range(QH_DEV):
        rows = pl.ds(h * TOK, TOK)
        phi_q = both_softmax(dot_nn(q_ref[h], fq_ref[h]), 1)
        phi_k = both_softmax(dot_nt(fkt_ref[h], keys), 0)
        kernel = jnp.where(causal, dot_nn(phi_q, phi_k), 0.0)
        phi_ref[rows, :] = phi_q
        numer_ref[rows, :] = dot_nn(kernel.astype(BF16), vals)
        denom_ref[rows, :] = jnp.broadcast_to(jnp.sum(kernel, axis=1, keepdims=True), (TOK, HD))
        rows_ref[pl.ds(h * BLOCK, BLOCK), :] = q_ref[h, pl.ds(pl.multiple_of(picked * BLOCK, BLOCK), BLOCK), :]
    scores = dot_nt(keys, rows_ref[...]) * SCORE_SCALE
    place = picked * BLOCK + lax.rem(lax.broadcasted_iota(jnp.int32, scores.shape, 1), BLOCK)
    live = lax.broadcasted_iota(jnp.int32, scores.shape, 0) <= place
    scores = jnp.where(live, scores, MASKED)
    best = jnp.max(scores, axis=0, keepdims=True)
    weights = jnp.exp2(scores - best)
    best_ref[...] = best
    total_ref[...] = jnp.sum(weights, axis=0, keepdims=True)
    accum_ref[...] = dot_tn(vals, weights.astype(BF16))


def own_part(samples, q, k, v, fq, fkt):
    vmem = pl.BlockSpec(memory_space=pltpu.VMEM)
    return pl.pallas_call(
        own_kernel,
        out_shape=(
            jax.ShapeDtypeStruct((QH_DEV * TOK, 2 * FEAT), BF16),
            jax.ShapeDtypeStruct((QH_DEV * TOK, HD), F32),
            jax.ShapeDtypeStruct((QH_DEV * TOK, HD), F32),
            jax.ShapeDtypeStruct((ROWS, HD), BF16),
            jax.ShapeDtypeStruct((1, ROWS), F32),
            jax.ShapeDtypeStruct((1, ROWS), F32),
            jax.ShapeDtypeStruct((HD, ROWS), F32),
        ),
        in_specs=[pl.BlockSpec(memory_space=pltpu.SMEM)] + [vmem] * 5,
        out_specs=(vmem,) * 7,
        compiler_params=pltpu.CompilerParams(vmem_limit_bytes=OWN_VMEM),
        cost_estimate=pl.CostEstimate(flops=OWN_COST * 10**6, transcendentals=10**6, bytes_accessed=2**21),
    )(samples, q, k, v, fq, fkt)


def take_in(fkt_ref, rows_ref, old, pieces, best_ref, total_ref, accum_ref, state_ref,
            first_ref, second_ref, scores_ref, where):
    y, z = position()
    mine = y * NZ + z
    blocks = scores_ref.shape[0] // TOK
    live = [where(i, y, z) < mine for i in range(blocks)]
    some = functools.reduce(jnp.logical_or, live)
    if old[3] is None:
        state_ref[...] = jnp.zeros(state_ref.shape, F32)
    else:
        state_ref[...] = old[3][...]

    @pl.when(jnp.logical_not(some))
    def _():
        best_ref[...] = old[0][...]
        total_ref[...] = old[1][...]
        accum_ref[...] = old[2][...]

    def go(buffer, weights_ref, phi_ref):
        begin = 0
        for piece in pieces:
            buffer[pl.ds(begin, piece.shape[0]), :] = piece[...]
            begin += piece.shape[0]

        def span(i):
            return pl.ds(pl.multiple_of(i * TOK, TOK), TOK)

        def logits(i, to):
            keys = buffer[span(i), :HD]
            for h in range(QH_DEV):
                to[h] = dot_nt(fkt_ref[h], keys)

        def score(i, top):
            scores = dot_nt(buffer[span(i), :HD], rows_ref[...])
            scores_ref[span(i), :] = scores
            peak = jnp.max(scores.reshape(TOK // 8, 8, ROWS), axis=0)
            return jnp.maximum(top, jnp.where(where(i, y, z) < mine, peak, MASKED))

        def feature(i, out_of):
            keep = jnp.where(where(i, y, z) < mine, 1.0, 0.0).astype(F32)
            for h in range(QH_DEV):
                for half in range(2):
                    part = out_of[h, :, half * 128:(half + 1) * 128]
                    up = jnp.exp(part - jnp.max(part, axis=0, keepdims=True))
                    down = jnp.exp(jnp.min(part, axis=0, keepdims=True) - part)
                    up = up * (keep / jnp.sum(up, axis=0, keepdims=True))
                    down = down * (keep / jnp.sum(down, axis=0, keepdims=True))
                    to = pl.ds(pl.multiple_of(i * TOK, TOK) + half * 128, 128)
                    phi_ref[pl.ds(h * 2 * FEAT, FEAT), to] = up.astype(BF16)
                    phi_ref[pl.ds(h * 2 * FEAT + FEAT, FEAT), to] = down.astype(BF16)

        logits(0, first_ref)

        def two(j, top):
            i = 2 * j
            logits(i + 1, second_ref)
            feature(i, first_ref)
            top = score(i, top)
            logits(jnp.minimum(i + 2, blocks - 1), first_ref)
            feature(i + 1, second_ref)
            return score(i + 1, top)

        top = lax.fori_loop(0, blocks // 2, two, jnp.full((8, ROWS), MASKED, F32))
        if blocks % 2:
            feature(blocks - 1, first_ref)
            top = score(blocks - 1, top)
        best = old[0][...]
        newtop = jnp.maximum(best, jnp.max(top, axis=0, keepdims=True) * SCORE_SCALE)
        fade = jnp.exp2(best - newtop)
        best_ref[...] = newtop
        sums = jnp.zeros((8, ROWS), F32)
        ones = jnp.ones((blocks * TOK, HD), BF16)
        wide = jnp.concatenate([buffer[:, HD:], ones], axis=1)
        state_ref[...] = state_ref[...] + dot_nn(phi_ref[...], wide)
        for i in range(blocks):
            shift = jnp.where(live[i], newtop, -MASKED)
            weights = jnp.exp2(scores_ref[pl.ds(i * TOK, TOK), :] * SCORE_SCALE - shift)
            sums = sums + jnp.sum(weights.reshape(TOK // 8, 8, ROWS), axis=0)
            weights_ref[pl.ds(i * TOK, TOK), :] = weights.astype(BF16)
        total_ref[...] = fade * old[1][...] + jnp.sum(sums, axis=0, keepdims=True)
        accum_ref[...] = fade * old[2][...] + dot_tn(buffer[:, HD:], weights_ref[...])

    @pl.when(some)
    def _():
        pl.run_scoped(
            go,
            pltpu.VMEM((blocks * TOK, 2 * HD), BF16),
            pltpu.VMEM((blocks * TOK, ROWS), BF16),
            pltpu.VMEM((QH_DEV * 2 * FEAT, blocks * TOK), BF16),
        )


def work_space(blocks):
    return [
        pltpu.VMEM((QH_DEV, FEAT, TOK), F32),
        pltpu.VMEM((QH_DEV, FEAT, TOK), F32),
        pltpu.VMEM((blocks * TOK, ROWS), F32),
    ]


CARRY = (
    jax.ShapeDtypeStruct((1, ROWS), F32),
    jax.ShapeDtypeStruct((1, ROWS), F32),
    jax.ShapeDtypeStruct((HD, ROWS), F32),
    jax.ShapeDtypeStruct((QH_DEV * 2 * FEAT, 2 * HD), F32),
)


def absorb_kernel(fkt_ref, rows_ref, *refs, where, parts, fresh):
    carried = 3 if fresh else 4
    old = refs[:3] + ((None,) if fresh else (refs[3],))
    pieces = refs[carried:carried + parts]
    take_in(fkt_ref, rows_ref, old, pieces, *refs[carried + parts:], where)


def absorb(fkt, rows, carry, pieces, where):
    vmem = pl.BlockSpec(memory_space=pltpu.VMEM)
    fresh = len(carry) == 3
    return pl.pallas_call(
        functools.partial(absorb_kernel, where=where, parts=len(pieces), fresh=fresh),
        out_shape=CARRY,
        in_specs=[vmem] * (2 + len(carry) + len(pieces)),
        out_specs=(vmem,) * 4,
        scratch_shapes=work_space(sum(p.shape[0] for p in pieces) // TOK),
        compiler_params=pltpu.CompilerParams(vmem_limit_bytes=VMEM),
        cost_estimate=pl.CostEstimate(flops=COST * 10**6, transcendentals=10**6, bytes_accessed=2**21),
    )(fkt, rows, *carry, *pieces)


def last_kernel(samples_ref, fkt_ref, rows_ref, *refs, where, parts):
    old, pieces, refs = refs[:4], refs[4:4 + parts], refs[4 + parts:]
    phi_ref, numer_ref, denom_ref, student_ref, teacher_ref, square_ref, keep = refs[:7]
    carry = refs[7:11]
    take_in(fkt_ref, rows_ref, old, pieces, *refs[7:], where)
    total_ref, accum_ref, state_ref = carry[1:]
    y, z = position()
    picked = samples_ref[y * NZ + z]
    for h in range(QH_DEV):
        rows = pl.ds(h * TOK, TOK)
        state = state_ref[pl.ds(h * 2 * FEAT, 2 * FEAT), :].astype(BF16)
        across = dot_nn(phi_ref[rows, :], state)
        ratio = (numer_ref[rows, :] + across[:, :HD]) / (denom_ref[rows, :] + across[:, HD:])
        ratio = ratio.astype(BF16)
        student_ref[h] = ratio
        keep[h] = ratio.astype(F32)
    mixed = jnp.transpose(accum_ref[...] / total_ref[...])
    squares = jnp.zeros((BLOCK, HD), F32)
    for h in range(QH_DEV):
        teacher = mixed[h * BLOCK:(h + 1) * BLOCK]
        teacher_ref[h] = teacher
        gap = keep[h, pl.ds(pl.multiple_of(picked * BLOCK, BLOCK), BLOCK), :] - teacher
        squares = squares + gap * gap
    square_ref[...] = jnp.full(square_ref.shape, jnp.sum(squares), F32)


def last_part(samples, fkt, rows, carry, pieces, where, phi, numer, denom, group):
    vmem = pl.BlockSpec(memory_space=pltpu.VMEM)
    return pl.pallas_call(
        functools.partial(last_kernel, where=where, parts=len(pieces)),
        out_shape=(
            jax.ShapeDtypeStruct((QH_DEV, TOK, HD), BF16),
            jax.ShapeDtypeStruct((QH_DEV, BLOCK, HD), F32),
            jax.ShapeDtypeStruct((group, 1, 128), F32),
        ),
        in_specs=[pl.BlockSpec(memory_space=pltpu.SMEM)] + [vmem] * (9 + len(pieces)),
        out_specs=(vmem,) * 3,
        scratch_shapes=[pltpu.VMEM((QH_DEV, TOK, HD), F32)]
        + [pltpu.VMEM(c.shape, c.dtype) for c in CARRY]
        + work_space(sum(p.shape[0] for p in pieces) // TOK),
        compiler_params=pltpu.CompilerParams(vmem_limit_bytes=VMEM),
    )(samples, fkt, rows, *carry, *pieces, phi, numer, denom)


def along_z(x, step):
    return lax.ppermute(x, "z", [(z, (z + step) % NZ) for z in range(NZ)])


def listed(*blocks):
    def place(block, y, z):
        row, step = block
        column = lax.rem(z + NZ - step, NZ)
        if row is None:
            return y * NZ + column
        return jnp.where(y == row, NY * NZ, row * NZ + column)

    def where(i, y, z):
        if isinstance(i, int):
            return place(blocks[i], y, z)
        found = place(blocks[0], y, z)
        for n in range(1, len(blocks)):
            found = jnp.where(i == n, place(blocks[n], y, z), found)
        return found

    return where


def earlier(step):
    return tuple((row, step) for row in range(NY - 1))


def on_device(queries, keys, values, feat_q, feat_k, samples):
    group = lax.axis_size("y") * lax.axis_size("z") * lax.axis_size("head")
    own = jnp.concatenate([keys[:, 0], values[:, 0]], axis=1)
    near = [along_z(own, step) for step in (1, -1)]
    far = [along_z(own, step) for step in (2, -2)]
    column = lax.all_to_all(jnp.broadcast_to(own[None], (NY,) + own.shape), "y", 0, 0)
    column = column.reshape(NY * TOK, 2 * HD)[: (NY - 1) * TOK]
    q = jnp.transpose(queries, (1, 0, 2))
    fkt = jnp.transpose(feat_k, (0, 2, 1))
    phi, numer, denom, rows, *carry = own_part(samples, q, keys[:, 0], values[:, 0], feat_q, fkt)
    up = along_z(jnp.concatenate([column, far[0]], axis=0), 1)
    down = along_z(jnp.concatenate([far[1], column], axis=0), -1)
    carry = absorb(fkt, rows, carry, [column], listed(*earlier(0)))
    carry = absorb(
        fkt, rows, carry, near + far, listed((None, 1), (None, -1), (None, 2), (None, -2))
    )
    first = [up, down]
    half = TOK // 2
    up, down = along_z(up[:-half], 1), along_z(down[half:], -1)
    carry = absorb(
        fkt, rows, carry, first,
        listed(*earlier(1), (None, 3), (None, -3), *earlier(-1)),
    )
    second = [up, down]
    up, down = along_z(up[:-half], 1), along_z(down[half:], -1)
    carry = absorb(fkt, rows, carry, second, listed(*earlier(2), (None, 4), *earlier(-2)))
    third = [up, down]
    half = up.shape[0] // 2
    up, down = along_z(up[:half], 1), along_z(down[half:], -1)
    carry = absorb(fkt, rows, carry, third, listed(*earlier(3), *earlier(-3)))
    student, teacher, square = last_part(
        samples, fkt, rows, carry, [up, down], listed(*earlier(4)), phi, numer, denom, group
    )
    shared = lax.all_to_all(square, ("y", "z", "head"), 0, 0)
    loss = jnp.sum(shared[:, 0, 0]) / (group * BLOCK * QH_DEV * HD)
    return (
        jnp.transpose(student, (1, 0, 2)),
        jnp.transpose(teacher, (1, 0, 2))[None],
        loss,
    )


def solution(mesh):
    head = mesh.shape["head"]
    torus = Mesh(mesh.devices.reshape(NY, NZ, head), ("y", "z", "head"))
    seq = ("y", "z")
    in_specs = (
        P(seq, "head", None),
        P(seq, "head", None),
        P(seq, "head", None),
        P("head", None, None),
        P("head", None, None),
        P(),
    )
    out_specs = (P(seq, "head", None), P(seq, None, "head", None), P())
    return jax.shard_map(
        on_device, mesh=torus, in_specs=in_specs, out_specs=out_specs, check_vma=False
    )
```

```python
import functools

import jax
import jax.numpy as jnp
from jax import lax
from jax.experimental import pallas as pl
from jax.experimental.pallas import tpu as pltpu
from jax.sharding import Mesh, PartitionSpec as P

HD = 128
FEAT = 128
QH_DEV = 4
BLOCK = 128
TOK = 256
ROWS = QH_DEV * BLOCK
NY = 4
NZ = 8
MASKED = -1e30
COST = 10000
OWN_VMEM = 12 * 2**20
VMEM = 28 * 2**20
OWN_COST = 1000
F32 = jnp.float32
BF16 = jnp.bfloat16
LOG2E = 1.4426950408889634
SCORE_SCALE = LOG2E / HD**0.5


def dot_nn(a, b):
    return lax.dot_general(a, b, (((1,), (0,)), ((), ())), preferred_element_type=F32)


def dot_nt(a, b):
    return lax.dot_general(a, b, (((1,), (1,)), ((), ())), preferred_element_type=F32)


def dot_tn(a, b):
    return lax.dot_general(a, b, (((0,), (0,)), ((), ())), preferred_element_type=F32)


def both_softmax(logits, axis):
    up = jnp.exp(logits - jnp.max(logits, axis=axis, keepdims=True))
    down = jnp.exp(jnp.min(logits, axis=axis, keepdims=True) - logits)
    up = up * (1.0 / jnp.sum(up, axis=axis, keepdims=True))
    down = down * (1.0 / jnp.sum(down, axis=axis, keepdims=True))
    return jnp.concatenate([up, down], axis=axis).astype(BF16)


def position():
    return lax.axis_index("y"), lax.axis_index("z")


def own_kernel(samples_ref, after_ref, q_ref, k_ref, v_ref, fq_ref, fkt_ref,
               phi_ref, numer_ref, denom_ref, rows_ref, best_ref, total_ref, accum_ref):
    y, z = position()
    picked = samples_ref[y * NZ + z]
    keys = k_ref[...]
    vals = v_ref[...]
    causal = lax.broadcasted_iota(jnp.int32, (TOK, TOK), 0) >= lax.broadcasted_iota(
        jnp.int32, (TOK, TOK), 1
    )
    for h in range(QH_DEV):
        rows = pl.ds(h * TOK, TOK)
        phi_q = both_softmax(dot_nn(q_ref[h], fq_ref[h]), 1)
        phi_k = both_softmax(dot_nt(fkt_ref[h], keys), 0)
        kernel = jnp.where(causal, dot_nn(phi_q, phi_k), 0.0)
        phi_ref[rows, :] = phi_q
        numer_ref[rows, :] = dot_nn(kernel.astype(BF16), vals)
        denom_ref[rows, :] = jnp.broadcast_to(jnp.sum(kernel, axis=1, keepdims=True), (TOK, HD))
        rows_ref[pl.ds(h * BLOCK, BLOCK), :] = q_ref[h, pl.ds(pl.multiple_of(picked * BLOCK, BLOCK), BLOCK), :]
    scores = dot_nt(keys, rows_ref[...]) * SCORE_SCALE
    place = picked * BLOCK + lax.rem(lax.broadcasted_iota(jnp.int32, scores.shape, 1), BLOCK)
    live = lax.broadcasted_iota(jnp.int32, scores.shape, 0) <= place
    scores = jnp.where(live, scores, MASKED)
    best = jnp.max(scores, axis=0, keepdims=True)
    weights = jnp.exp2(scores - best)
    best_ref[...] = best
    total_ref[...] = jnp.sum(weights, axis=0, keepdims=True)
    accum_ref[...] = dot_tn(vals, weights.astype(BF16))


def own_part(samples, after, q, k, v, fq, fkt):
    vmem = pl.BlockSpec(memory_space=pltpu.VMEM)
    return pl.pallas_call(
        own_kernel,
        out_shape=(
            jax.ShapeDtypeStruct((QH_DEV * TOK, 2 * FEAT), BF16),
            jax.ShapeDtypeStruct((QH_DEV * TOK, HD), F32),
            jax.ShapeDtypeStruct((QH_DEV * TOK, HD), F32),
            jax.ShapeDtypeStruct((ROWS, HD), BF16),
            jax.ShapeDtypeStruct((1, ROWS), F32),
            jax.ShapeDtypeStruct((1, ROWS), F32),
            jax.ShapeDtypeStruct((HD, ROWS), F32),
        ),
        in_specs=[pl.BlockSpec(memory_space=pltpu.SMEM), pl.BlockSpec(memory_space=pl.ANY)] + [vmem] * 5,
        out_specs=(vmem,) * 7,
        compiler_params=pltpu.CompilerParams(vmem_limit_bytes=OWN_VMEM),
        cost_estimate=pl.CostEstimate(flops=OWN_COST * 10**6, transcendentals=10**6, bytes_accessed=2**21),
    )(samples, after, q, k, v, fq, fkt)


def take_in(fkt_ref, rows_ref, old, pieces, best_ref, total_ref, accum_ref, state_ref,
            first_ref, second_ref, scores_ref, where):
    y, z = position()
    mine = y * NZ + z
    blocks = scores_ref.shape[0] // TOK
    live = [where(i, y, z) < mine for i in range(blocks)]
    some = functools.reduce(jnp.logical_or, live)
    if old[3] is None:
        state_ref[...] = jnp.zeros(state_ref.shape, F32)
    else:
        state_ref[...] = old[3][...]

    @pl.when(jnp.logical_not(some))
    def _():
        best_ref[...] = old[0][...]
        total_ref[...] = old[1][...]
        accum_ref[...] = old[2][...]

    def go(buffer, weights_ref, phi_ref):
        begin = 0
        for piece in pieces:
            buffer[pl.ds(begin, piece.shape[0]), :] = piece[...]
            begin += piece.shape[0]

        def span(i):
            return pl.ds(pl.multiple_of(i * TOK, TOK), TOK)

        def logits(i, to):
            keys = buffer[span(i), :HD]
            for h in range(QH_DEV):
                to[h] = dot_nt(fkt_ref[h], keys)

        def score(i, top):
            scores = dot_nt(buffer[span(i), :HD], rows_ref[...])
            scores_ref[span(i), :] = scores
            peak = jnp.max(scores.reshape(TOK // 8, 8, ROWS), axis=0)
            return jnp.maximum(top, jnp.where(where(i, y, z) < mine, peak, MASKED))

        def feature(i, out_of):
            keep = jnp.where(where(i, y, z) < mine, 1.0, 0.0).astype(F32)
            for h in range(QH_DEV):
                for half in range(2):
                    part = out_of[h, :, half * 128:(half + 1) * 128]
                    up = jnp.exp(part - jnp.max(part, axis=0, keepdims=True))
                    down = jnp.exp(jnp.min(part, axis=0, keepdims=True) - part)
                    up = up * (keep / jnp.sum(up, axis=0, keepdims=True))
                    down = down * (keep / jnp.sum(down, axis=0, keepdims=True))
                    to = pl.ds(pl.multiple_of(i * TOK, TOK) + half * 128, 128)
                    phi_ref[pl.ds(h * 2 * FEAT, FEAT), to] = up.astype(BF16)
                    phi_ref[pl.ds(h * 2 * FEAT + FEAT, FEAT), to] = down.astype(BF16)

        logits(0, first_ref)

        def two(j, top):
            i = 2 * j
            logits(i + 1, second_ref)
            feature(i, first_ref)
            top = score(i, top)
            logits(jnp.minimum(i + 2, blocks - 1), first_ref)
            feature(i + 1, second_ref)
            return score(i + 1, top)

        top = lax.fori_loop(0, blocks // 2, two, jnp.full((8, ROWS), MASKED, F32))
        if blocks % 2:
            feature(blocks - 1, first_ref)
            top = score(blocks - 1, top)
        best = old[0][...]
        newtop = jnp.maximum(best, jnp.max(top, axis=0, keepdims=True) * SCORE_SCALE)
        fade = jnp.exp2(best - newtop)
        best_ref[...] = newtop
        sums = jnp.zeros((8, ROWS), F32)
        ones = jnp.ones((blocks * TOK, HD), BF16)
        wide = jnp.concatenate([buffer[:, HD:], ones], axis=1)
        state_ref[...] = state_ref[...] + dot_nn(phi_ref[...], wide)
        for i in range(blocks):
            shift = jnp.where(live[i], newtop, -MASKED)
            weights = jnp.exp2(scores_ref[pl.ds(i * TOK, TOK), :] * SCORE_SCALE - shift)
            sums = sums + jnp.sum(weights.reshape(TOK // 8, 8, ROWS), axis=0)
            weights_ref[pl.ds(i * TOK, TOK), :] = weights.astype(BF16)
        total_ref[...] = fade * old[1][...] + jnp.sum(sums, axis=0, keepdims=True)
        accum_ref[...] = fade * old[2][...] + dot_tn(buffer[:, HD:], weights_ref[...])

    @pl.when(some)
    def _():
        pl.run_scoped(
            go,
            pltpu.VMEM((blocks * TOK, 2 * HD), BF16),
            pltpu.VMEM((blocks * TOK, ROWS), BF16),
            pltpu.VMEM((QH_DEV * 2 * FEAT, blocks * TOK), BF16),
        )


def work_space(blocks):
    return [
        pltpu.VMEM((QH_DEV, FEAT, TOK), F32),
        pltpu.VMEM((QH_DEV, FEAT, TOK), F32),
        pltpu.VMEM((blocks * TOK, ROWS), F32),
    ]


CARRY = (
    jax.ShapeDtypeStruct((1, ROWS), F32),
    jax.ShapeDtypeStruct((1, ROWS), F32),
    jax.ShapeDtypeStruct((HD, ROWS), F32),
    jax.ShapeDtypeStruct((QH_DEV * 2 * FEAT, 2 * HD), F32),
)


def absorb_kernel(fkt_ref, rows_ref, *refs, where, parts, fresh):
    carried = 3 if fresh else 4
    old = refs[:3] + ((None,) if fresh else (refs[3],))
    pieces = refs[carried:carried + parts]
    take_in(fkt_ref, rows_ref, old, pieces, *refs[carried + parts:], where)


def absorb(fkt, rows, carry, pieces, where):
    vmem = pl.BlockSpec(memory_space=pltpu.VMEM)
    fresh = len(carry) == 3
    return pl.pallas_call(
        functools.partial(absorb_kernel, where=where, parts=len(pieces), fresh=fresh),
        out_shape=CARRY,
        in_specs=[vmem] * (2 + len(carry) + len(pieces)),
        out_specs=(vmem,) * 4,
        scratch_shapes=work_space(sum(p.shape[0] for p in pieces) // TOK),
        compiler_params=pltpu.CompilerParams(vmem_limit_bytes=VMEM),
        cost_estimate=pl.CostEstimate(flops=COST * 10**6, transcendentals=10**6, bytes_accessed=2**21),
    )(fkt, rows, *carry, *pieces)


def last_kernel(samples_ref, fkt_ref, rows_ref, *refs, where, parts):
    old, pieces, refs = refs[:4], refs[4:4 + parts], refs[4 + parts:]
    phi_ref, numer_ref, denom_ref, student_ref, teacher_ref, square_ref, keep = refs[:7]
    carry = refs[7:11]
    take_in(fkt_ref, rows_ref, old, pieces, *refs[7:], where)
    total_ref, accum_ref, state_ref = carry[1:]
    y, z = position()
    picked = samples_ref[y * NZ + z]
    for h in range(QH_DEV):
        rows = pl.ds(h * TOK, TOK)
        state = state_ref[pl.ds(h * 2 * FEAT, 2 * FEAT), :].astype(BF16)
        across = dot_nn(phi_ref[rows, :], state)
        ratio = (numer_ref[rows, :] + across[:, :HD]) / (denom_ref[rows, :] + across[:, HD:])
        ratio = ratio.astype(BF16)
        student_ref[h] = ratio
        keep[h] = ratio.astype(F32)
    mixed = jnp.transpose(accum_ref[...] / total_ref[...])
    squares = jnp.zeros((BLOCK, HD), F32)
    for h in range(QH_DEV):
        teacher = mixed[h * BLOCK:(h + 1) * BLOCK]
        teacher_ref[h] = teacher
        gap = keep[h, pl.ds(pl.multiple_of(picked * BLOCK, BLOCK), BLOCK), :] - teacher
        squares = squares + gap * gap
    square_ref[...] = jnp.full(square_ref.shape, jnp.sum(squares), F32)


def last_part(samples, fkt, rows, carry, pieces, where, phi, numer, denom, group):
    vmem = pl.BlockSpec(memory_space=pltpu.VMEM)
    return pl.pallas_call(
        functools.partial(last_kernel, where=where, parts=len(pieces)),
        out_shape=(
            jax.ShapeDtypeStruct((QH_DEV, TOK, HD), BF16),
            jax.ShapeDtypeStruct((QH_DEV, BLOCK, HD), F32),
            jax.ShapeDtypeStruct((group, 1, 128), F32),
        ),
        in_specs=[pl.BlockSpec(memory_space=pltpu.SMEM)] + [vmem] * (9 + len(pieces)),
        out_specs=(vmem,) * 3,
        scratch_shapes=[pltpu.VMEM((QH_DEV, TOK, HD), F32)]
        + [pltpu.VMEM(c.shape, c.dtype) for c in CARRY]
        + work_space(sum(p.shape[0] for p in pieces) // TOK),
        compiler_params=pltpu.CompilerParams(vmem_limit_bytes=VMEM),
    )(samples, fkt, rows, *carry, *pieces, phi, numer, denom)


def spread_kernel(k_ref, v_ref, own_ref, wide_ref):
    pair = jnp.concatenate([k_ref[...], v_ref[...]], axis=1)
    own_ref[...] = pair
    for row in range(NY):
        wide_ref[row] = pair


def spread(k, v):
    vmem = pl.BlockSpec(memory_space=pltpu.VMEM)
    return pl.pallas_call(
        spread_kernel,
        out_shape=(
            jax.ShapeDtypeStruct((TOK, 2 * HD), BF16),
            jax.ShapeDtypeStruct((NY, TOK, 2 * HD), BF16),
        ),
        in_specs=[vmem] * 2,
        out_specs=(vmem,) * 2,
        compiler_params=pltpu.CompilerParams(vmem_limit_bytes=4 * 2**20),
    )(k, v)


def along_z(x, step):
    return lax.ppermute(x, "z", [(z, (z + step) % NZ) for z in range(NZ)])


def listed(*blocks):
    def place(block, y, z):
        row, step = block
        column = lax.rem(z + NZ - step, NZ)
        if row is None:
            return y * NZ + column
        return jnp.where(y == row, NY * NZ, row * NZ + column)

    def where(i, y, z):
        if isinstance(i, int):
            return place(blocks[i], y, z)
        found = place(blocks[0], y, z)
        for n in range(1, len(blocks)):
            found = jnp.where(i == n, place(blocks[n], y, z), found)
        return found

    return where


def earlier(step):
    return tuple((row, step) for row in range(NY - 1))


def on_device(queries, keys, values, feat_q, feat_k, samples):
    group = lax.axis_size("y") * lax.axis_size("z") * lax.axis_size("head")
    k, v = (pltpu.with_memory_space_constraint(a[:, 0], pltpu.HBM) for a in (keys, values))
    own, wide = spread(k, v)
    near = [along_z(own, step) for step in (1, -1)]
    far = [along_z(own, step) for step in (2, -2)]
    column = lax.all_to_all(wide, "y", 0, 0)
    column = column.reshape(NY * TOK, 2 * HD)[: (NY - 1) * TOK]
    q = jnp.transpose(queries, (1, 0, 2))
    fkt = jnp.transpose(feat_k, (0, 2, 1))
    phi, numer, denom, rows, *carry = own_part(
        samples, column, q, k, v, feat_q, fkt
    )
    up = along_z(jnp.concatenate([column, far[0]], axis=0), 1)
    down = along_z(jnp.concatenate([far[1], column], axis=0), -1)
    carry = absorb(fkt, rows, carry, [column], listed(*earlier(0)))
    carry = absorb(
        fkt, rows, carry, near + far, listed((None, 1), (None, -1), (None, 2), (None, -2))
    )
    first = [up, down]
    half = TOK // 2
    up, down = along_z(up[:-half], 1), along_z(down[half:], -1)
    carry = absorb(
        fkt, rows, carry, first,
        listed(*earlier(1), (None, 3), (None, -3), *earlier(-1)),
    )
    second = [up, down]
    up, down = along_z(up[:-half], 1), along_z(down[half:], -1)
    carry = absorb(fkt, rows, carry, second, listed(*earlier(2), (None, 4), *earlier(-2)))
    third = [up, down]
    half = up.shape[0] // 2
    up, down = along_z(up[:half], 1), along_z(down[half:], -1)
    carry = absorb(fkt, rows, carry, third, listed(*earlier(3), *earlier(-3)))
    student, teacher, square = last_part(
        samples, fkt, rows, carry, [up, down], listed(*earlier(4)), phi, numer, denom, group
    )
    shared = lax.all_to_all(square, ("y", "z", "head"), 0, 0)
    loss = jnp.sum(shared[:, 0, 0]) / (group * BLOCK * QH_DEV * HD)
    return (
        jnp.transpose(student, (1, 0, 2)),
        jnp.transpose(teacher, (1, 0, 2))[None],
        loss,
    )


def solution(mesh):
    head = mesh.shape["head"]
    torus = Mesh(mesh.devices.reshape(NY, NZ, head), ("y", "z", "head"))
    seq = ("y", "z")
    in_specs = (
        P(seq, "head", None),
        P(seq, "head", None),
        P(seq, "head", None),
        P("head", None, None),
        P("head", None, None),
        P(),
    )
    out_specs = (P(seq, "head", None), P(seq, None, "head", None), P())
    return jax.shard_map(
        on_device, mesh=torus, in_specs=in_specs, out_specs=out_specs, check_vma=False
    )
```

```python
import functools

import jax
import jax.numpy as jnp
from jax import lax
from jax.experimental import pallas as pl
from jax.experimental.pallas import tpu as pltpu
from jax.sharding import Mesh, PartitionSpec as P

HD = 128
FEAT = 128
QH_DEV = 4
BLOCK = 128
TOK = 256
ROWS = QH_DEV * BLOCK
NY = 4
NZ = 8
MASKED = -1e30
COST = 10000
OWN_VMEM = 12 * 2**20
VMEM = 28 * 2**20
HELP_COST = 10000
OWN_COST = 1000
F32 = jnp.float32
BF16 = jnp.bfloat16
LOG2E = 1.4426950408889634
SCORE_SCALE = LOG2E / HD**0.5


def dot_nn(a, b):
    return lax.dot_general(a, b, (((1,), (0,)), ((), ())), preferred_element_type=F32)


def dot_nt(a, b):
    return lax.dot_general(a, b, (((1,), (1,)), ((), ())), preferred_element_type=F32)


def dot_tn(a, b):
    return lax.dot_general(a, b, (((0,), (0,)), ((), ())), preferred_element_type=F32)


def both_softmax(logits, axis):
    up = jnp.exp(logits - jnp.max(logits, axis=axis, keepdims=True))
    down = jnp.exp(jnp.min(logits, axis=axis, keepdims=True) - logits)
    up = up * (1.0 / jnp.sum(up, axis=axis, keepdims=True))
    down = down * (1.0 / jnp.sum(down, axis=axis, keepdims=True))
    return jnp.concatenate([up, down], axis=axis).astype(BF16)


def position():
    return lax.axis_index("y"), lax.axis_index("z")


def own_kernel(samples_ref, q_ref, k_ref, v_ref, fq_ref, fkt_ref,
               phi_ref, numer_ref, denom_ref, rows_ref, best_ref, total_ref, accum_ref):
    y, z = position()
    picked = samples_ref[y * NZ + z]
    keys = k_ref[...]
    vals = v_ref[...]
    causal = lax.broadcasted_iota(jnp.int32, (TOK, TOK), 0) >= lax.broadcasted_iota(
        jnp.int32, (TOK, TOK), 1
    )
    for h in range(QH_DEV):
        rows = pl.ds(h * TOK, TOK)
        phi_q = both_softmax(dot_nn(q_ref[h], fq_ref[h]), 1)
        phi_k = both_softmax(dot_nt(fkt_ref[h], keys), 0)
        kernel = jnp.where(causal, dot_nn(phi_q, phi_k), 0.0)
        phi_ref[rows, :] = phi_q
        numer_ref[rows, :] = dot_nn(kernel.astype(BF16), vals)
        denom_ref[rows, :] = jnp.broadcast_to(jnp.sum(kernel, axis=1, keepdims=True), (TOK, HD))
        rows_ref[pl.ds(h * BLOCK, BLOCK), :] = q_ref[h, pl.ds(pl.multiple_of(picked * BLOCK, BLOCK), BLOCK), :]
    scores = dot_nt(keys, rows_ref[...]) * SCORE_SCALE
    place = picked * BLOCK + lax.rem(lax.broadcasted_iota(jnp.int32, scores.shape, 1), BLOCK)
    live = lax.broadcasted_iota(jnp.int32, scores.shape, 0) <= place
    scores = jnp.where(live, scores, MASKED)
    best = jnp.max(scores, axis=0, keepdims=True)
    weights = jnp.exp2(scores - best)
    best_ref[...] = best
    total_ref[...] = jnp.sum(weights, axis=0, keepdims=True)
    accum_ref[...] = dot_tn(vals, weights.astype(BF16))


def own_part(samples, q, k, v, fq, fkt):
    vmem = pl.BlockSpec(memory_space=pltpu.VMEM)
    return pl.pallas_call(
        own_kernel,
        out_shape=(
            jax.ShapeDtypeStruct((QH_DEV * TOK, 2 * FEAT), BF16),
            jax.ShapeDtypeStruct((QH_DEV * TOK, HD), F32),
            jax.ShapeDtypeStruct((QH_DEV * TOK, HD), F32),
            jax.ShapeDtypeStruct((ROWS, HD), BF16),
            jax.ShapeDtypeStruct((1, ROWS), F32),
            jax.ShapeDtypeStruct((1, ROWS), F32),
            jax.ShapeDtypeStruct((HD, ROWS), F32),
        ),
        in_specs=[pl.BlockSpec(memory_space=pltpu.SMEM)] + [vmem] * 5,
        out_specs=(vmem,) * 7,
        compiler_params=pltpu.CompilerParams(vmem_limit_bytes=OWN_VMEM),
        cost_estimate=pl.CostEstimate(flops=OWN_COST * 10**6, transcendentals=10**6, bytes_accessed=2**21),
    )(samples, q, k, v, fq, fkt)


def take_in(fkt_ref, rows_ref, old, pieces, best_ref, total_ref, accum_ref, state_ref,
            first_ref, second_ref, scores_ref, where):
    y, z = position()
    mine = y * NZ + z
    blocks = scores_ref.shape[0] // TOK
    live = [where(i, y, z) < mine for i in range(blocks)]
    some = functools.reduce(jnp.logical_or, live)
    if old[3] is None:
        state_ref[...] = jnp.zeros(state_ref.shape, F32)
    else:
        state_ref[...] = old[3][...]

    if old[0] is not None:

        @pl.when(jnp.logical_not(some))
        def _():
            best_ref[...] = old[0][...]
            total_ref[...] = old[1][...]
            accum_ref[...] = old[2][...]

    def go(buffer, weights_ref, phi_ref):
        begin = 0
        for piece, (start, size) in pieces:
            buffer[pl.ds(begin, size), :] = piece[pl.ds(start, size), :]
            begin += size

        def span(i):
            return pl.ds(pl.multiple_of(i * TOK, TOK), TOK)

        def logits(i, to):
            keys = buffer[span(i), :HD]
            for h in range(QH_DEV):
                to[h] = dot_nt(fkt_ref[h], keys)

        def score(i, top):
            scores = dot_nt(buffer[span(i), :HD], rows_ref[...])
            scores_ref[span(i), :] = scores
            peak = jnp.max(scores.reshape(TOK // 8, 8, ROWS), axis=0)
            return jnp.maximum(top, jnp.where(where(i, y, z) < mine, peak, MASKED))

        def feature(i, out_of):
            keep = jnp.where(where(i, y, z) < mine, 1.0, 0.0).astype(F32)
            for h in range(QH_DEV):
                for half in range(2):
                    part = out_of[h, :, half * 128:(half + 1) * 128]
                    up = jnp.exp(part - jnp.max(part, axis=0, keepdims=True))
                    down = jnp.exp(jnp.min(part, axis=0, keepdims=True) - part)
                    up = up * (keep / jnp.sum(up, axis=0, keepdims=True))
                    down = down * (keep / jnp.sum(down, axis=0, keepdims=True))
                    to = pl.ds(pl.multiple_of(i * TOK, TOK) + half * 128, 128)
                    phi_ref[pl.ds(h * 2 * FEAT, FEAT), to] = up.astype(BF16)
                    phi_ref[pl.ds(h * 2 * FEAT + FEAT, FEAT), to] = down.astype(BF16)

        logits(0, first_ref)

        def two(j, top):
            i = 2 * j
            logits(i + 1, second_ref)
            feature(i, first_ref)
            top = score(i, top)
            logits(jnp.minimum(i + 2, blocks - 1), first_ref)
            feature(i + 1, second_ref)
            return score(i + 1, top)

        top = lax.fori_loop(0, blocks // 2, two, jnp.full((8, ROWS), MASKED, F32))
        if blocks % 2:
            feature(blocks - 1, first_ref)
            top = score(blocks - 1, top)
        best = jnp.full((1, ROWS), MASKED, F32) if old[0] is None else old[0][...]
        newtop = jnp.maximum(best, jnp.max(top, axis=0, keepdims=True) * SCORE_SCALE)
        fade = jnp.exp2(best - newtop)
        best_ref[...] = newtop
        sums = jnp.zeros((8, ROWS), F32)
        ones = jnp.ones((blocks * TOK, HD), BF16)
        wide = jnp.concatenate([buffer[:, HD:], ones], axis=1)
        state_ref[...] = state_ref[...] + dot_nn(phi_ref[...], wide)
        for i in range(blocks):
            shift = jnp.where(live[i], newtop, -MASKED)
            weights = jnp.exp2(scores_ref[pl.ds(i * TOK, TOK), :] * SCORE_SCALE - shift)
            sums = sums + jnp.sum(weights.reshape(TOK // 8, 8, ROWS), axis=0)
            weights_ref[pl.ds(i * TOK, TOK), :] = weights.astype(BF16)
        total = jnp.sum(sums, axis=0, keepdims=True)
        accum = dot_tn(buffer[:, HD:], weights_ref[...])
        total_ref[...] = total if old[1] is None else fade * old[1][...] + total
        accum_ref[...] = accum if old[2] is None else fade * old[2][...] + accum

    @pl.when(some)
    def _():
        pl.run_scoped(
            go,
            pltpu.VMEM((blocks * TOK, 2 * HD), BF16),
            pltpu.VMEM((blocks * TOK, ROWS), BF16),
            pltpu.VMEM((QH_DEV * 2 * FEAT, blocks * TOK), BF16),
        )


def work_space(blocks):
    return [
        pltpu.VMEM((QH_DEV, FEAT, TOK), F32),
        pltpu.VMEM((QH_DEV, FEAT, TOK), F32),
        pltpu.VMEM((blocks * TOK, ROWS), F32),
    ]


CARRY = (
    jax.ShapeDtypeStruct((1, ROWS), F32),
    jax.ShapeDtypeStruct((1, ROWS), F32),
    jax.ShapeDtypeStruct((HD, ROWS), F32),
    jax.ShapeDtypeStruct((QH_DEV * 2 * FEAT, 2 * HD), F32),
)


def absorb_kernel(fkt_ref, rows_ref, *refs, where, windows, fresh):
    carried = 3 if fresh else 4
    old = refs[:3] + ((None,) if fresh else (refs[3],))
    parts = len(windows)
    pieces = tuple(zip(refs[carried:carried + parts], windows))
    take_in(fkt_ref, rows_ref, old, pieces, *refs[carried + parts:], where)


def whole(pieces):
    return tuple((0, p.shape[0]) for p in pieces)


def absorb(fkt, rows, carry, pieces, where):
    vmem = pl.BlockSpec(memory_space=pltpu.VMEM)
    fresh = len(carry) == 3
    return pl.pallas_call(
        functools.partial(absorb_kernel, where=where, windows=whole(pieces), fresh=fresh),
        out_shape=CARRY,
        in_specs=[vmem] * (2 + len(carry) + len(pieces)),
        out_specs=(vmem,) * 4,
        scratch_shapes=work_space(sum(p.shape[0] for p in pieces) // TOK),
        compiler_params=pltpu.CompilerParams(vmem_limit_bytes=VMEM),
        cost_estimate=pl.CostEstimate(flops=COST * 10**6, transcendentals=10**6, bytes_accessed=2**21),
    )(fkt, rows, *carry, *pieces)


def help_kernel(fkt_ref, rows_ref, *refs, where, windows):
    parts = len(windows)
    pieces = tuple(zip(refs[:parts], windows))
    sums_ref, packed_ref = refs[parts:parts + 2]
    best_ref, total_ref, accum_ref, state_ref = refs[parts + 2:parts + 6]
    take_in(fkt_ref, rows_ref, (None,) * 4, pieces, *refs[parts + 2:], where)

    @pl.when(lax.axis_index("y") == 0)
    def _():
        sums_ref[pl.ds(0, 1), :] = best_ref[...]
        sums_ref[pl.ds(1, 1), :] = total_ref[...]
        across = jnp.transpose(state_ref[:, HD:])
        sums_ref[pl.ds(2, 1), :] = across[:1, :ROWS]
        sums_ref[pl.ds(3, 1), :] = across[:1, ROWS:]
        sums_ref[pl.ds(4, 4), :] = jnp.zeros((4, ROWS), F32)
        packed_ref[pl.ds(0, QH_DEV * 2 * FEAT), :] = state_ref[:, :HD].astype(BF16)
        for h in range(QH_DEV):
            packed_ref[pl.ds(QH_DEV * 2 * FEAT + h * HD, HD), :] = accum_ref[
                :, h * BLOCK:(h + 1) * BLOCK
            ].astype(BF16)


def help_last_row(fkt, rows, pieces, windows):
    vmem = pl.BlockSpec(memory_space=pltpu.VMEM)
    blocks = sum(size for _, size in windows) // TOK
    return pl.pallas_call(
        functools.partial(
            help_kernel, windows=windows, where=lambda i, y, z: jnp.where(y == 0, -1, NY * NZ)
        ),
        out_shape=(
            jax.ShapeDtypeStruct((8, ROWS), F32),
            jax.ShapeDtypeStruct((QH_DEV * 2 * FEAT + ROWS, HD), BF16),
        ),
        in_specs=[vmem] * (2 + len(pieces)),
        out_specs=(vmem,) * 2,
        scratch_shapes=[pltpu.VMEM(c.shape, c.dtype) for c in CARRY] + work_space(blocks),
        compiler_params=pltpu.CompilerParams(vmem_limit_bytes=VMEM),
        cost_estimate=pl.CostEstimate(flops=HELP_COST * 10**6, transcendentals=10**6, bytes_accessed=2**21),
    )(fkt, rows, *pieces)


def last_kernel(samples_ref, fkt_ref, rows_ref, *refs, where, windows):
    parts = len(windows)
    old, pieces, refs = refs[:4], tuple(zip(refs[4:4 + parts], windows)), refs[4 + parts:]
    sums_ref, packed_ref, phi_ref, numer_ref, denom_ref, student_ref, teacher_ref, square_ref, keep = refs[:9]
    carry = refs[9:13]
    take_in(fkt_ref, rows_ref, old, pieces, *refs[9:], where)
    best_ref, total_ref, accum_ref, state_ref = carry
    y, z = position()
    picked = samples_ref[y * NZ + z]
    for h in range(QH_DEV):
        rows = pl.ds(h * TOK, TOK)
        here = pl.ds(h * 2 * FEAT, 2 * FEAT)
        first = (state_ref[here, :HD] + packed_ref[here, :].astype(F32)).astype(BF16)
        state = jnp.concatenate([first, state_ref[here, HD:].astype(BF16)], axis=1)
        across = dot_nn(phi_ref[rows, :], state)
        more = sums_ref[pl.ds(2 + h // 2, 1), pl.ds((h % 2) * 2 * FEAT, 2 * FEAT)]
        more = dot_nt(phi_ref[rows, :], jnp.broadcast_to(more, (HD, 2 * FEAT)).astype(BF16))
        ratio = (numer_ref[rows, :] + across[:, :HD]) / (denom_ref[rows, :] + across[:, HD:] + more)
        ratio = ratio.astype(BF16)
        student_ref[h] = ratio
        keep[h] = ratio.astype(F32)
    best = best_ref[...]
    other = jnp.where(y == NY - 1, sums_ref[pl.ds(0, 1), :], MASKED)
    newtop = jnp.maximum(best, other)
    fade = jnp.exp2(best - newtop)
    rise = jnp.exp2(other - newtop)
    total = fade * total_ref[...] + rise * sums_ref[pl.ds(1, 1), :]
    squares = jnp.zeros((BLOCK, HD), F32)
    for h in range(QH_DEV):
        cols = slice(h * BLOCK, (h + 1) * BLOCK)
        added = packed_ref[pl.ds(QH_DEV * 2 * FEAT + h * HD, HD), :].astype(F32)
        mixed = (fade[:, cols] * accum_ref[:, cols] + rise[:, cols] * added) / total[:, cols]
        teacher = jnp.transpose(mixed)
        teacher_ref[h] = teacher
        gap = keep[h, pl.ds(pl.multiple_of(picked * BLOCK, BLOCK), BLOCK), :] - teacher
        squares = squares + gap * gap
    square_ref[...] = jnp.full(square_ref.shape, jnp.sum(squares), F32)


def last_part(samples, fkt, rows, carry, pieces, where, helped, phi, numer, denom, group):
    vmem = pl.BlockSpec(memory_space=pltpu.VMEM)
    return pl.pallas_call(
        functools.partial(last_kernel, where=where, windows=whole(pieces)),
        out_shape=(
            jax.ShapeDtypeStruct((QH_DEV, TOK, HD), BF16),
            jax.ShapeDtypeStruct((QH_DEV, BLOCK, HD), F32),
            jax.ShapeDtypeStruct((group, 1, 128), F32),
        ),
        in_specs=[pl.BlockSpec(memory_space=pltpu.SMEM)] + [vmem] * (11 + len(pieces)),
        out_specs=(vmem,) * 3,
        scratch_shapes=[pltpu.VMEM((QH_DEV, TOK, HD), F32)]
        + [pltpu.VMEM(c.shape, c.dtype) for c in CARRY]
        + work_space(sum(p.shape[0] for p in pieces) // TOK),
        compiler_params=pltpu.CompilerParams(vmem_limit_bytes=VMEM),
    )(samples, fkt, rows, *carry, *pieces, *helped, phi, numer, denom)


def join_kernel(k_ref, v_ref, own_ref):
    own_ref[:, :HD] = k_ref[...]
    own_ref[:, HD:] = v_ref[...]


def join(k, v):
    vmem = pl.BlockSpec(memory_space=pltpu.VMEM)
    return pl.pallas_call(
        join_kernel,
        out_shape=jax.ShapeDtypeStruct((TOK, 2 * HD), BF16),
        in_specs=[vmem] * 2,
        out_specs=vmem,
        compiler_params=pltpu.CompilerParams(vmem_limit_bytes=4 * 2**20),
    )(k, v)


def along_z(x, step):
    return lax.ppermute(x, "z", [(z, (z + step) % NZ) for z in range(NZ)])


def along_y(x, step, least=0):
    return lax.ppermute(x, "y", [(y, y + step) for y in range(NY) if least <= y and 0 <= y + step < NY])


def listed(*blocks):
    def place(block, y, z):
        back, step = block
        column = (y - back) * NZ + lax.rem(z + NZ - step, NZ)
        return column if back == 0 else jnp.where(y < back, NY * NZ, column)

    def where(i, y, z):
        if isinstance(i, int):
            return place(blocks[i], y, z)
        found = place(blocks[0], y, z)
        for n in range(1, len(blocks)):
            found = jnp.where(i == n, place(blocks[n], y, z), found)
        return found

    return where


def earlier(step):
    return ((1, step), (2, step))


def on_device(queries, keys, values, feat_q, feat_k, samples):
    group = lax.axis_size("y") * lax.axis_size("z") * lax.axis_size("head")
    k, v = (pltpu.with_memory_space_constraint(a[:, 0], pltpu.HBM) for a in (keys, values))
    own = join(k, v)
    far = [along_z(own, step) for step in (2, -2)]
    column = jnp.concatenate([along_y(own, 1), along_y(own, 2)], axis=0)
    near = [along_z(own, step) for step in (1, -1)]
    q = jnp.transpose(queries, (1, 0, 2))
    fkt = jnp.transpose(feat_k, (0, 2, 1))
    phi, numer, denom, rows, *carry = own_part(samples, q, k, v, feat_q, fkt)
    asked = along_y(rows, 1 - NY)
    up = along_z(jnp.concatenate([column, far[0]], axis=0), 1)
    down = along_z(jnp.concatenate([far[1], column], axis=0), -1)
    carry = absorb(fkt, rows, carry, [column], listed(*earlier(0)))
    carry = absorb(fkt, rows, carry, near + far, listed((0, 1), (0, -1), (0, 2), (0, -2)))
    first = [up, down]
    half = TOK // 2
    helped = help_last_row(
        fkt, asked, [own, *near, *far, up, down],
        ((0, TOK),) * 5 + ((2 * TOK, TOK), (0, TOK)),
    )
    helped = [along_y(a, NY - 1) for a in helped]
    up, down = along_z(up[:-half], 1), along_z(down[half:], -1)
    carry = absorb(fkt, rows, carry, first, listed(*earlier(1), (0, 3), (0, -3), *earlier(-1)))
    second = [up, down]
    opposite = along_y(jnp.concatenate([up[-half:], down[:half]], axis=0), NY - 1)
    up, down = along_z(up[:-half], 1), along_z(down[half:], -1)
    carry = absorb(fkt, rows, carry, second, listed(*earlier(2), (0, 4), *earlier(-2)))
    third = [up, down]
    up, down = along_z(up[:TOK], 1), along_z(down[TOK:], -1)
    carry = absorb(fkt, rows, carry, third, listed(*earlier(3), *earlier(-3)))
    student, teacher, square = last_part(
        samples, fkt, rows, carry, [up, down, opposite], listed((1, 4), (2, 4), (3, 4)),
        helped, phi, numer, denom, group,
    )
    shared = lax.all_to_all(square, ("y", "z", "head"), 0, 0)
    loss = jnp.sum(shared[:, 0, 0]) / (group * BLOCK * QH_DEV * HD)
    return (
        jnp.transpose(student, (1, 0, 2)),
        jnp.transpose(teacher, (1, 0, 2))[None],
        loss,
    )


def solution(mesh):
    head = mesh.shape["head"]
    torus = Mesh(mesh.devices.reshape(NY, NZ, head), ("y", "z", "head"))
    seq = ("y", "z")
    in_specs = (
        P(seq, "head", None),
        P(seq, "head", None),
        P(seq, "head", None),
        P("head", None, None),
        P("head", None, None),
        P(),
    )
    out_specs = (P(seq, "head", None), P(seq, None, "head", None), P())
    return jax.shard_map(
        on_device, mesh=torus, in_specs=in_specs, out_specs=out_specs, check_vma=False
    )
```

```python
import functools

import jax
import jax.numpy as jnp
from jax import lax
from jax.experimental import pallas as pl
from jax.experimental.pallas import tpu as pltpu
from jax.sharding import Mesh, PartitionSpec as P

HD = 128
FEAT = 128
QH_DEV = 4
BLOCK = 128
TOK = 256
ROWS = QH_DEV * BLOCK
NY = 4
NZ = 8
MASKED = -1e30
COST = 10000
OWN_VMEM = 12 * 2**20
VMEM = 28 * 2**20
HELP_COST = 10000
OWN_COST = 1000
F32 = jnp.float32
BF16 = jnp.bfloat16
LOG2E = 1.4426950408889634
SCORE_SCALE = LOG2E / HD**0.5


def dot_nn(a, b):
    return lax.dot_general(a, b, (((1,), (0,)), ((), ())), preferred_element_type=F32)


def dot_nt(a, b):
    return lax.dot_general(a, b, (((1,), (1,)), ((), ())), preferred_element_type=F32)


def dot_tn(a, b):
    return lax.dot_general(a, b, (((0,), (0,)), ((), ())), preferred_element_type=F32)


def both_softmax(logits, axis):
    up = jnp.exp(logits - jnp.max(logits, axis=axis, keepdims=True))
    down = jnp.exp(jnp.min(logits, axis=axis, keepdims=True) - logits)
    up = up * (1.0 / jnp.sum(up, axis=axis, keepdims=True))
    down = down * (1.0 / jnp.sum(down, axis=axis, keepdims=True))
    return jnp.concatenate([up, down], axis=axis).astype(BF16)


def position():
    return lax.axis_index("y"), lax.axis_index("z")


def own_kernel(samples_ref, after_ref, q_ref, k_ref, v_ref, fq_ref, fkt_ref,
               phi_ref, numer_ref, denom_ref, rows_ref, best_ref, total_ref, accum_ref):
    y, z = position()
    picked = samples_ref[y * NZ + z]
    keys = k_ref[...]
    vals = v_ref[...]
    causal = lax.broadcasted_iota(jnp.int32, (TOK, TOK), 0) >= lax.broadcasted_iota(
        jnp.int32, (TOK, TOK), 1
    )
    for h in range(QH_DEV):
        rows = pl.ds(h * TOK, TOK)
        phi_q = both_softmax(dot_nn(q_ref[h], fq_ref[h]), 1)
        phi_k = both_softmax(dot_nt(fkt_ref[h], keys), 0)
        kernel = jnp.where(causal, dot_nn(phi_q, phi_k), 0.0)
        phi_ref[rows, :] = phi_q
        numer_ref[rows, :] = dot_nn(kernel.astype(BF16), vals)
        denom_ref[rows, :] = jnp.broadcast_to(jnp.sum(kernel, axis=1, keepdims=True), (TOK, HD))
        rows_ref[pl.ds(h * BLOCK, BLOCK), :] = q_ref[h, pl.ds(pl.multiple_of(picked * BLOCK, BLOCK), BLOCK), :]
    scores = dot_nt(keys, rows_ref[...]) * SCORE_SCALE
    place = picked * BLOCK + lax.rem(lax.broadcasted_iota(jnp.int32, scores.shape, 1), BLOCK)
    live = lax.broadcasted_iota(jnp.int32, scores.shape, 0) <= place
    scores = jnp.where(live, scores, MASKED)
    best = jnp.max(scores, axis=0, keepdims=True)
    weights = jnp.exp2(scores - best)
    best_ref[...] = best
    total_ref[...] = jnp.sum(weights, axis=0, keepdims=True)
    accum_ref[...] = dot_tn(vals, weights.astype(BF16))


def own_part(samples, after, q, k, v, fq, fkt):
    vmem = pl.BlockSpec(memory_space=pltpu.VMEM)
    return pl.pallas_call(
        own_kernel,
        out_shape=(
            jax.ShapeDtypeStruct((QH_DEV * TOK, 2 * FEAT), BF16),
            jax.ShapeDtypeStruct((QH_DEV * TOK, HD), F32),
            jax.ShapeDtypeStruct((QH_DEV * TOK, HD), F32),
            jax.ShapeDtypeStruct((ROWS, HD), BF16),
            jax.ShapeDtypeStruct((1, ROWS), F32),
            jax.ShapeDtypeStruct((1, ROWS), F32),
            jax.ShapeDtypeStruct((HD, ROWS), F32),
        ),
        in_specs=[pl.BlockSpec(memory_space=pltpu.SMEM), pl.BlockSpec(memory_space=pl.ANY)] + [vmem] * 5,
        out_specs=(vmem,) * 7,
        compiler_params=pltpu.CompilerParams(vmem_limit_bytes=OWN_VMEM),
        cost_estimate=pl.CostEstimate(flops=OWN_COST * 10**6, transcendentals=10**6, bytes_accessed=2**21),
    )(samples, after, q, k, v, fq, fkt)


def take_in(fkt_ref, rows_ref, old, pieces, best_ref, total_ref, accum_ref, state_ref,
            first_ref, second_ref, scores_ref, where):
    y, z = position()
    mine = y * NZ + z
    blocks = scores_ref.shape[0] // TOK
    live = [where(i, y, z) < mine for i in range(blocks)]
    some = functools.reduce(jnp.logical_or, live)
    if old[3] is None:
        state_ref[...] = jnp.zeros(state_ref.shape, F32)
    else:
        state_ref[...] = old[3][...]

    if old[0] is not None:

        @pl.when(jnp.logical_not(some))
        def _():
            best_ref[...] = old[0][...]
            total_ref[...] = old[1][...]
            accum_ref[...] = old[2][...]

    def go(buffer, weights_ref, phi_ref):
        begin = 0
        for piece, (start, size) in pieces:
            buffer[pl.ds(begin, size), :] = piece[pl.ds(start, size), :]
            begin += size

        def span(i):
            return pl.ds(pl.multiple_of(i * TOK, TOK), TOK)

        def logits(i, to):
            keys = buffer[span(i), :HD]
            for h in range(QH_DEV):
                to[h] = dot_nt(fkt_ref[h], keys)

        def score(i, top):
            scores = dot_nt(buffer[span(i), :HD], rows_ref[...])
            scores_ref[span(i), :] = scores
            peak = jnp.max(scores.reshape(TOK // 8, 8, ROWS), axis=0)
            return jnp.maximum(top, jnp.where(where(i, y, z) < mine, peak, MASKED))

        def feature(i, out_of):
            keep = jnp.where(where(i, y, z) < mine, 1.0, 0.0).astype(F32)
            for h in range(QH_DEV):
                for half in range(2):
                    part = out_of[h, :, half * 128:(half + 1) * 128]
                    up = jnp.exp(part - jnp.max(part, axis=0, keepdims=True))
                    down = jnp.exp(jnp.min(part, axis=0, keepdims=True) - part)
                    up = up * (keep / jnp.sum(up, axis=0, keepdims=True))
                    down = down * (keep / jnp.sum(down, axis=0, keepdims=True))
                    to = pl.ds(pl.multiple_of(i * TOK, TOK) + half * 128, 128)
                    phi_ref[pl.ds(h * 2 * FEAT, FEAT), to] = up.astype(BF16)
                    phi_ref[pl.ds(h * 2 * FEAT + FEAT, FEAT), to] = down.astype(BF16)

        logits(0, first_ref)

        def two(j, top):
            i = 2 * j
            logits(i + 1, second_ref)
            feature(i, first_ref)
            top = score(i, top)
            logits(jnp.minimum(i + 2, blocks - 1), first_ref)
            feature(i + 1, second_ref)
            return score(i + 1, top)

        top = lax.fori_loop(0, blocks // 2, two, jnp.full((8, ROWS), MASKED, F32))
        if blocks % 2:
            feature(blocks - 1, first_ref)
            top = score(blocks - 1, top)
        best = jnp.full((1, ROWS), MASKED, F32) if old[0] is None else old[0][...]
        newtop = jnp.maximum(best, jnp.max(top, axis=0, keepdims=True) * SCORE_SCALE)
        fade = jnp.exp2(best - newtop)
        best_ref[...] = newtop
        sums = jnp.zeros((8, ROWS), F32)
        ones = jnp.ones((blocks * TOK, HD), BF16)
        wide = jnp.concatenate([buffer[:, HD:], ones], axis=1)
        state_ref[...] = state_ref[...] + dot_nn(phi_ref[...], wide)
        for i in range(blocks):
            shift = jnp.where(live[i], newtop, -MASKED)
            weights = jnp.exp2(scores_ref[pl.ds(i * TOK, TOK), :] * SCORE_SCALE - shift)
            sums = sums + jnp.sum(weights.reshape(TOK // 8, 8, ROWS), axis=0)
            weights_ref[pl.ds(i * TOK, TOK), :] = weights.astype(BF16)
        total = jnp.sum(sums, axis=0, keepdims=True)
        accum = dot_tn(buffer[:, HD:], weights_ref[...])
        total_ref[...] = total if old[1] is None else fade * old[1][...] + total
        accum_ref[...] = accum if old[2] is None else fade * old[2][...] + accum

    @pl.when(some)
    def _():
        pl.run_scoped(
            go,
            pltpu.VMEM((blocks * TOK, 2 * HD), BF16),
            pltpu.VMEM((blocks * TOK, ROWS), BF16),
            pltpu.VMEM((QH_DEV * 2 * FEAT, blocks * TOK), BF16),
        )


def work_space(blocks):
    return [
        pltpu.VMEM((QH_DEV, FEAT, TOK), F32),
        pltpu.VMEM((QH_DEV, FEAT, TOK), F32),
        pltpu.VMEM((blocks * TOK, ROWS), F32),
    ]


CARRY = (
    jax.ShapeDtypeStruct((1, ROWS), F32),
    jax.ShapeDtypeStruct((1, ROWS), F32),
    jax.ShapeDtypeStruct((HD, ROWS), F32),
    jax.ShapeDtypeStruct((QH_DEV * 2 * FEAT, 2 * HD), F32),
)


def absorb_kernel(fkt_ref, rows_ref, *refs, where, windows, fresh):
    carried = 3 if fresh else 4
    old = refs[:3] + ((None,) if fresh else (refs[3],))
    parts = len(windows)
    pieces = tuple(zip(refs[carried:carried + parts], windows))
    take_in(fkt_ref, rows_ref, old, pieces, *refs[carried + parts:], where)


def whole(pieces):
    return tuple((0, p.shape[0]) for p in pieces)


def absorb(fkt, rows, carry, pieces, where):
    vmem = pl.BlockSpec(memory_space=pltpu.VMEM)
    fresh = len(carry) == 3
    return pl.pallas_call(
        functools.partial(absorb_kernel, where=where, windows=whole(pieces), fresh=fresh),
        out_shape=CARRY,
        in_specs=[vmem] * (2 + len(carry) + len(pieces)),
        out_specs=(vmem,) * 4,
        scratch_shapes=work_space(sum(p.shape[0] for p in pieces) // TOK),
        compiler_params=pltpu.CompilerParams(vmem_limit_bytes=VMEM),
        cost_estimate=pl.CostEstimate(flops=COST * 10**6, transcendentals=10**6, bytes_accessed=2**21),
    )(fkt, rows, *carry, *pieces)


def help_kernel(fkt_ref, rows_ref, *refs, where, windows):
    parts = len(windows)
    pieces = tuple(zip(refs[:parts], windows))
    sums_ref, packed_ref = refs[parts:parts + 2]
    best_ref, total_ref, accum_ref, state_ref = refs[parts + 2:parts + 6]
    take_in(fkt_ref, rows_ref, (None,) * 4, pieces, *refs[parts + 2:], where)

    @pl.when(lax.axis_index("y") == 0)
    def _():
        sums_ref[pl.ds(0, 1), :] = best_ref[...]
        sums_ref[pl.ds(1, 1), :] = total_ref[...]
        across = jnp.transpose(state_ref[:, HD:])
        sums_ref[pl.ds(2, 1), :] = across[:1, :ROWS]
        sums_ref[pl.ds(3, 1), :] = across[:1, ROWS:]
        sums_ref[pl.ds(4, 4), :] = jnp.zeros((4, ROWS), F32)
        packed_ref[pl.ds(0, QH_DEV * 2 * FEAT), :] = state_ref[:, :HD].astype(BF16)
        for h in range(QH_DEV):
            packed_ref[pl.ds(QH_DEV * 2 * FEAT + h * HD, HD), :] = accum_ref[
                :, h * BLOCK:(h + 1) * BLOCK
            ].astype(BF16)


def help_last_row(fkt, rows, pieces, windows):
    vmem = pl.BlockSpec(memory_space=pltpu.VMEM)
    blocks = sum(size for _, size in windows) // TOK
    return pl.pallas_call(
        functools.partial(
            help_kernel, windows=windows, where=lambda i, y, z: jnp.where(y == 0, -1, NY * NZ)
        ),
        out_shape=(
            jax.ShapeDtypeStruct((8, ROWS), F32),
            jax.ShapeDtypeStruct((QH_DEV * 2 * FEAT + ROWS, HD), BF16),
        ),
        in_specs=[vmem] * (2 + len(pieces)),
        out_specs=(vmem,) * 2,
        scratch_shapes=[pltpu.VMEM(c.shape, c.dtype) for c in CARRY] + work_space(blocks),
        compiler_params=pltpu.CompilerParams(vmem_limit_bytes=VMEM),
        cost_estimate=pl.CostEstimate(flops=HELP_COST * 10**6, transcendentals=10**6, bytes_accessed=2**21),
    )(fkt, rows, *pieces)


def last_kernel(samples_ref, fkt_ref, rows_ref, *refs, where, windows):
    parts = len(windows)
    old, pieces, refs = refs[:4], tuple(zip(refs[4:4 + parts], windows)), refs[4 + parts:]
    sums_ref, packed_ref, phi_ref, numer_ref, denom_ref, student_ref, teacher_ref, square_ref, keep = refs[:9]
    carry = refs[9:13]
    take_in(fkt_ref, rows_ref, old, pieces, *refs[9:], where)
    best_ref, total_ref, accum_ref, state_ref = carry
    y, z = position()
    picked = samples_ref[y * NZ + z]
    for h in range(QH_DEV):
        rows = pl.ds(h * TOK, TOK)
        here = pl.ds(h * 2 * FEAT, 2 * FEAT)
        first = (state_ref[here, :HD] + packed_ref[here, :].astype(F32)).astype(BF16)
        state = jnp.concatenate([first, state_ref[here, HD:].astype(BF16)], axis=1)
        across = dot_nn(phi_ref[rows, :], state)
        more = sums_ref[pl.ds(2 + h // 2, 1), pl.ds((h % 2) * 2 * FEAT, 2 * FEAT)]
        more = dot_nt(phi_ref[rows, :], jnp.broadcast_to(more, (HD, 2 * FEAT)).astype(BF16))
        ratio = (numer_ref[rows, :] + across[:, :HD]) / (denom_ref[rows, :] + across[:, HD:] + more)
        ratio = ratio.astype(BF16)
        student_ref[h] = ratio
        keep[h] = ratio.astype(F32)
    best = best_ref[...]
    other = jnp.where(y == NY - 1, sums_ref[pl.ds(0, 1), :], MASKED)
    newtop = jnp.maximum(best, other)
    fade = jnp.exp2(best - newtop)
    rise = jnp.exp2(other - newtop)
    total = fade * total_ref[...] + rise * sums_ref[pl.ds(1, 1), :]
    squares = jnp.zeros((BLOCK, HD), F32)
    for h in range(QH_DEV):
        cols = slice(h * BLOCK, (h + 1) * BLOCK)
        added = packed_ref[pl.ds(QH_DEV * 2 * FEAT + h * HD, HD), :].astype(F32)
        mixed = (fade[:, cols] * accum_ref[:, cols] + rise[:, cols] * added) / total[:, cols]
        teacher = jnp.transpose(mixed)
        teacher_ref[h] = teacher
        gap = keep[h, pl.ds(pl.multiple_of(picked * BLOCK, BLOCK), BLOCK), :] - teacher
        squares = squares + gap * gap
    square_ref[...] = jnp.full(square_ref.shape, jnp.sum(squares), F32)


def last_part(samples, fkt, rows, carry, pieces, where, helped, phi, numer, denom, group):
    vmem = pl.BlockSpec(memory_space=pltpu.VMEM)
    return pl.pallas_call(
        functools.partial(last_kernel, where=where, windows=whole(pieces)),
        out_shape=(
            jax.ShapeDtypeStruct((QH_DEV, TOK, HD), BF16),
            jax.ShapeDtypeStruct((QH_DEV, BLOCK, HD), F32),
            jax.ShapeDtypeStruct((group, 1, 128), F32),
        ),
        in_specs=[pl.BlockSpec(memory_space=pltpu.SMEM)] + [vmem] * (11 + len(pieces)),
        out_specs=(vmem,) * 3,
        scratch_shapes=[pltpu.VMEM((QH_DEV, TOK, HD), F32)]
        + [pltpu.VMEM(c.shape, c.dtype) for c in CARRY]
        + work_space(sum(p.shape[0] for p in pieces) // TOK),
        compiler_params=pltpu.CompilerParams(vmem_limit_bytes=VMEM),
    )(samples, fkt, rows, *carry, *pieces, *helped, phi, numer, denom)


def join_kernel(k_ref, v_ref, own_ref):
    own_ref[:, :HD] = k_ref[...]
    own_ref[:, HD:] = v_ref[...]


def join(k, v):
    vmem = pl.BlockSpec(memory_space=pltpu.VMEM)
    return pl.pallas_call(
        join_kernel,
        out_shape=jax.ShapeDtypeStruct((TOK, 2 * HD), BF16),
        in_specs=[vmem] * 2,
        out_specs=vmem,
        compiler_params=pltpu.CompilerParams(vmem_limit_bytes=4 * 2**20),
    )(k, v)


def along_z(x, step):
    return lax.ppermute(x, "z", [(z, (z + step) % NZ) for z in range(NZ)])


def along_y(x, step, least=0):
    return lax.ppermute(x, "y", [(y, y + step) for y in range(NY) if least <= y and 0 <= y + step < NY])


def listed(*blocks):
    def place(block, y, z):
        back, step = block
        column = (y - back) * NZ + lax.rem(z + NZ - step, NZ)
        return column if back == 0 else jnp.where(y < back, NY * NZ, column)

    def where(i, y, z):
        if isinstance(i, int):
            return place(blocks[i], y, z)
        found = place(blocks[0], y, z)
        for n in range(1, len(blocks)):
            found = jnp.where(i == n, place(blocks[n], y, z), found)
        return found

    return where


def earlier(step):
    return ((1, step), (2, step))


def on_device(queries, keys, values, feat_q, feat_k, samples):
    group = lax.axis_size("y") * lax.axis_size("z") * lax.axis_size("head")
    k, v = (pltpu.with_memory_space_constraint(a[:, 0], pltpu.HBM) for a in (keys, values))
    own = join(k, v)
    far = [along_z(own, step) for step in (2, -2)]
    column = jnp.concatenate([along_y(own, 1), along_y(own, 2)], axis=0)
    near = [along_z(own, step) for step in (1, -1)]
    q = jnp.transpose(queries, (1, 0, 2))
    fkt = jnp.transpose(feat_k, (0, 2, 1))
    phi, numer, denom, rows, *carry = own_part(samples, column, q, k, v, feat_q, fkt)
    asked = along_y(rows, 1 - NY)
    up = along_z(jnp.concatenate([column, far[0]], axis=0), 1)
    down = along_z(jnp.concatenate([far[1], column], axis=0), -1)
    carry = absorb(fkt, rows, carry, [column], listed(*earlier(0)))
    carry = absorb(fkt, rows, carry, near + far, listed((0, 1), (0, -1), (0, 2), (0, -2)))
    first = [up, down]
    half = TOK // 2
    helped = help_last_row(
        fkt, asked, [own, *near, *far, up, down],
        ((0, TOK),) * 5 + ((2 * TOK, TOK), (0, TOK)),
    )
    helped = [along_y(a, NY - 1) for a in helped]
    up, down = along_z(up[:-half], 1), along_z(down[half:], -1)
    carry = absorb(fkt, rows, carry, first, listed(*earlier(1), (0, 3), (0, -3), *earlier(-1)))
    second = [up, down]
    opposite = along_y(jnp.concatenate([up[-half:], down[:half]], axis=0), NY - 1)
    up, down = along_z(up[:-half], 1), along_z(down[half:], -1)
    carry = absorb(fkt, rows, carry, second, listed(*earlier(2), (0, 4), *earlier(-2)))
    third = [up, down]
    up, down = along_z(up[:TOK], 1), along_z(down[TOK:], -1)
    carry = absorb(fkt, rows, carry, third, listed(*earlier(3), *earlier(-3)))
    student, teacher, square = last_part(
        samples, fkt, rows, carry, [up, down, opposite], listed((1, 4), (2, 4), (3, 4)),
        helped, phi, numer, denom, group,
    )
    shared = lax.all_to_all(square, ("y", "z", "head"), 0, 0)
    loss = jnp.sum(shared[:, 0, 0]) / (group * BLOCK * QH_DEV * HD)
    return (
        jnp.transpose(student, (1, 0, 2)),
        jnp.transpose(teacher, (1, 0, 2))[None],
        loss,
    )


def solution(mesh):
    head = mesh.shape["head"]
    torus = Mesh(mesh.devices.reshape(NY, NZ, head), ("y", "z", "head"))
    seq = ("y", "z")
    in_specs = (
        P(seq, "head", None),
        P(seq, "head", None),
        P(seq, "head", None),
        P("head", None, None),
        P("head", None, None),
        P(),
    )
    out_specs = (P(seq, "head", None), P(seq, None, "head", None), P())
    return jax.shard_map(
        on_device, mesh=torus, in_specs=in_specs, out_specs=out_specs, check_vma=False
    )
```

```python
import functools

import jax
import jax.numpy as jnp
from jax import lax
from jax.experimental import pallas as pl
from jax.experimental.pallas import tpu as pltpu
from jax.sharding import Mesh, PartitionSpec as P

HD = 128
FEAT = 128
QH_DEV = 4
BLOCK = 128
TOK = 256
ROWS = QH_DEV * BLOCK
NY = 4
NZ = 8
MASKED = -1e30
COST = 10000
OWN_VMEM = 12 * 2**20
VMEM = 28 * 2**20
HELP_COST = 10000
OWN_COST = 1000
F32 = jnp.float32
BF16 = jnp.bfloat16
LOG2E = 1.4426950408889634
SCORE_SCALE = LOG2E / HD**0.5


def dot_nn(a, b):
    return lax.dot_general(a, b, (((1,), (0,)), ((), ())), preferred_element_type=F32)


def dot_nt(a, b):
    return lax.dot_general(a, b, (((1,), (1,)), ((), ())), preferred_element_type=F32)


def dot_tn(a, b):
    return lax.dot_general(a, b, (((0,), (0,)), ((), ())), preferred_element_type=F32)


def both_softmax(logits, axis):
    up = jnp.exp(logits - jnp.max(logits, axis=axis, keepdims=True))
    down = jnp.exp(jnp.min(logits, axis=axis, keepdims=True) - logits)
    up = up * (1.0 / jnp.sum(up, axis=axis, keepdims=True))
    down = down * (1.0 / jnp.sum(down, axis=axis, keepdims=True))
    return jnp.concatenate([up, down], axis=axis).astype(BF16)


def position():
    return lax.axis_index("y"), lax.axis_index("z")


def own_kernel(samples_ref, after_ref, q_ref, k_ref, v_ref, fq_ref, fkt_ref,
               phi_ref, numer_ref, denom_ref, rows_ref, best_ref, total_ref, accum_ref):
    y, z = position()
    picked = samples_ref[y * NZ + z]
    keys = k_ref[...]
    vals = v_ref[...]
    causal = lax.broadcasted_iota(jnp.int32, (TOK, TOK), 0) >= lax.broadcasted_iota(
        jnp.int32, (TOK, TOK), 1
    )
    for h in range(QH_DEV):
        rows = pl.ds(h * TOK, TOK)
        phi_q = both_softmax(dot_nn(q_ref[h], fq_ref[h]), 1)
        phi_k = both_softmax(dot_nt(fkt_ref[h], keys), 0)
        kernel = jnp.where(causal, dot_nn(phi_q, phi_k), 0.0)
        phi_ref[rows, :] = phi_q
        numer_ref[rows, :] = dot_nn(kernel.astype(BF16), vals)
        denom_ref[rows, :] = jnp.broadcast_to(jnp.sum(kernel, axis=1, keepdims=True), (TOK, HD))
        rows_ref[pl.ds(h * BLOCK, BLOCK), :] = q_ref[h, pl.ds(pl.multiple_of(picked * BLOCK, BLOCK), BLOCK), :]
    scores = dot_nt(keys, rows_ref[...]) * SCORE_SCALE
    place = picked * BLOCK + lax.rem(lax.broadcasted_iota(jnp.int32, scores.shape, 1), BLOCK)
    live = lax.broadcasted_iota(jnp.int32, scores.shape, 0) <= place
    scores = jnp.where(live, scores, MASKED)
    best = jnp.max(scores, axis=0, keepdims=True)
    weights = jnp.exp2(scores - best)
    best_ref[...] = best
    total_ref[...] = jnp.sum(weights, axis=0, keepdims=True)
    accum_ref[...] = dot_tn(vals, weights.astype(BF16))


def own_part(samples, after, q, k, v, fq, fkt):
    vmem = pl.BlockSpec(memory_space=pltpu.VMEM)
    return pl.pallas_call(
        own_kernel,
        out_shape=(
            jax.ShapeDtypeStruct((QH_DEV * TOK, 2 * FEAT), BF16),
            jax.ShapeDtypeStruct((QH_DEV * TOK, HD), F32),
            jax.ShapeDtypeStruct((QH_DEV * TOK, HD), F32),
            jax.ShapeDtypeStruct((ROWS, HD), BF16),
            jax.ShapeDtypeStruct((1, ROWS), F32),
            jax.ShapeDtypeStruct((1, ROWS), F32),
            jax.ShapeDtypeStruct((HD, ROWS), F32),
        ),
        in_specs=[pl.BlockSpec(memory_space=pltpu.SMEM), pl.BlockSpec(memory_space=pl.ANY)] + [vmem] * 5,
        out_specs=(vmem,) * 7,
        compiler_params=pltpu.CompilerParams(vmem_limit_bytes=OWN_VMEM),
        cost_estimate=pl.CostEstimate(flops=OWN_COST * 10**6, transcendentals=10**6, bytes_accessed=2**21),
    )(samples, after, q, k, v, fq, fkt)


def take_in(fkt_ref, rows_ref, old, pieces, best_ref, total_ref, accum_ref, state_ref,
            first_ref, second_ref, scores_ref, where):
    y, z = position()
    mine = y * NZ + z
    blocks = scores_ref.shape[0] // TOK
    live = [where(i, y, z) < mine for i in range(blocks)]
    some = functools.reduce(jnp.logical_or, live)
    if old[3] is None:
        state_ref[...] = jnp.zeros(state_ref.shape, F32)
    else:
        state_ref[...] = old[3][...]

    if old[0] is not None:

        @pl.when(jnp.logical_not(some))
        def _():
            best_ref[...] = old[0][...]
            total_ref[...] = old[1][...]
            accum_ref[...] = old[2][...]

    def go(buffer, weights_ref, phi_ref):
        begin = 0
        for piece, (start, size) in pieces:
            buffer[pl.ds(begin, size), :] = piece[pl.ds(start, size), :]
            begin += size

        def span(i):
            return pl.ds(pl.multiple_of(i * TOK, TOK), TOK)

        def logits(i, to):
            keys = buffer[span(i), :HD]
            for h in range(QH_DEV):
                to[h] = dot_nt(fkt_ref[h], keys)

        def score(i, top):
            scores = dot_nt(buffer[span(i), :HD], rows_ref[...])
            scores_ref[span(i), :] = scores
            peak = jnp.max(scores.reshape(TOK // 8, 8, ROWS), axis=0)
            return jnp.maximum(top, jnp.where(where(i, y, z) < mine, peak, MASKED))

        def feature(i, out_of):
            keep = jnp.where(where(i, y, z) < mine, 1.0, 0.0).astype(F32)
            for h in range(QH_DEV):
                for half in range(2):
                    part = out_of[h, :, half * 128:(half + 1) * 128]
                    up = jnp.exp(part - jnp.max(part, axis=0, keepdims=True))
                    down = jnp.exp(jnp.min(part, axis=0, keepdims=True) - part)
                    up = up * (keep / jnp.sum(up, axis=0, keepdims=True))
                    down = down * (keep / jnp.sum(down, axis=0, keepdims=True))
                    to = pl.ds(pl.multiple_of(i * TOK, TOK) + half * 128, 128)
                    phi_ref[pl.ds(h * 2 * FEAT, FEAT), to] = up.astype(BF16)
                    phi_ref[pl.ds(h * 2 * FEAT + FEAT, FEAT), to] = down.astype(BF16)

        logits(0, first_ref)

        def two(j, top):
            i = 2 * j
            logits(i + 1, second_ref)
            feature(i, first_ref)
            top = score(i, top)
            logits(jnp.minimum(i + 2, blocks - 1), first_ref)
            feature(i + 1, second_ref)
            return score(i + 1, top)

        top = lax.fori_loop(0, blocks // 2, two, jnp.full((8, ROWS), MASKED, F32))
        if blocks % 2:
            feature(blocks - 1, first_ref)
            top = score(blocks - 1, top)
        best = jnp.full((1, ROWS), MASKED, F32) if old[0] is None else old[0][...]
        newtop = jnp.maximum(best, jnp.max(top, axis=0, keepdims=True) * SCORE_SCALE)
        fade = jnp.exp2(best - newtop)
        best_ref[...] = newtop
        sums = jnp.zeros((8, ROWS), F32)
        ones = jnp.ones((blocks * TOK, HD), BF16)
        wide = jnp.concatenate([buffer[:, HD:], ones], axis=1)
        state_ref[...] = state_ref[...] + dot_nn(phi_ref[...], wide)
        for i in range(blocks):
            shift = jnp.where(live[i], newtop, -MASKED)
            weights = jnp.exp2(scores_ref[pl.ds(i * TOK, TOK), :] * SCORE_SCALE - shift)
            sums = sums + jnp.sum(weights.reshape(TOK // 8, 8, ROWS), axis=0)
            weights_ref[pl.ds(i * TOK, TOK), :] = weights.astype(BF16)
        total = jnp.sum(sums, axis=0, keepdims=True)
        accum = dot_tn(buffer[:, HD:], weights_ref[...])
        total_ref[...] = total if old[1] is None else fade * old[1][...] + total
        accum_ref[...] = accum if old[2] is None else fade * old[2][...] + accum

    @pl.when(some)
    def _():
        pl.run_scoped(
            go,
            pltpu.VMEM((blocks * TOK, 2 * HD), BF16),
            pltpu.VMEM((blocks * TOK, ROWS), BF16),
            pltpu.VMEM((QH_DEV * 2 * FEAT, blocks * TOK), BF16),
        )


def work_space(blocks):
    return [
        pltpu.VMEM((QH_DEV, FEAT, TOK), F32),
        pltpu.VMEM((QH_DEV, FEAT, TOK), F32),
        pltpu.VMEM((blocks * TOK, ROWS), F32),
    ]


CARRY = (
    jax.ShapeDtypeStruct((1, ROWS), F32),
    jax.ShapeDtypeStruct((1, ROWS), F32),
    jax.ShapeDtypeStruct((HD, ROWS), F32),
    jax.ShapeDtypeStruct((QH_DEV * 2 * FEAT, 2 * HD), F32),
)


def absorb_kernel(fkt_ref, rows_ref, *refs, where, windows, fresh):
    carried = 3 if fresh else 4
    old = refs[:3] + ((None,) if fresh else (refs[3],))
    parts = len(windows)
    pieces = tuple(zip(refs[carried:carried + parts], windows))
    take_in(fkt_ref, rows_ref, old, pieces, *refs[carried + parts:], where)


def whole(pieces):
    return tuple((0, p.shape[0]) for p in pieces)


def absorb(fkt, rows, carry, pieces, where):
    vmem = pl.BlockSpec(memory_space=pltpu.VMEM)
    fresh = len(carry) == 3
    return pl.pallas_call(
        functools.partial(absorb_kernel, where=where, windows=whole(pieces), fresh=fresh),
        out_shape=CARRY,
        in_specs=[vmem] * (2 + len(carry) + len(pieces)),
        out_specs=(vmem,) * 4,
        scratch_shapes=work_space(sum(p.shape[0] for p in pieces) // TOK),
        compiler_params=pltpu.CompilerParams(vmem_limit_bytes=VMEM),
        cost_estimate=pl.CostEstimate(flops=COST * 10**6, transcendentals=10**6, bytes_accessed=2**21),
    )(fkt, rows, *carry, *pieces)


def help_kernel(fkt_ref, rows_ref, *refs, where, windows):
    parts = len(windows)
    pieces = tuple(zip(refs[:parts], windows))
    sums_ref, packed_ref = refs[parts:parts + 2]
    best_ref, total_ref, accum_ref, state_ref = refs[parts + 2:parts + 6]
    take_in(fkt_ref, rows_ref, (None,) * 4, pieces, *refs[parts + 2:], where)

    @pl.when(lax.axis_index("y") == 0)
    def _():
        sums_ref[pl.ds(0, 1), :] = best_ref[...]
        sums_ref[pl.ds(1, 1), :] = total_ref[...]
        across = jnp.transpose(state_ref[:, HD:])
        sums_ref[pl.ds(2, 1), :] = across[:1, :ROWS]
        sums_ref[pl.ds(3, 1), :] = across[:1, ROWS:]
        sums_ref[pl.ds(4, 4), :] = jnp.zeros((4, ROWS), F32)
        packed_ref[pl.ds(0, QH_DEV * 2 * FEAT), :] = state_ref[:, :HD].astype(BF16)
        for h in range(QH_DEV):
            packed_ref[pl.ds(QH_DEV * 2 * FEAT + h * HD, HD), :] = accum_ref[
                :, h * BLOCK:(h + 1) * BLOCK
            ].astype(BF16)


def help_last_row(fkt, rows, pieces, windows):
    vmem = pl.BlockSpec(memory_space=pltpu.VMEM)
    blocks = sum(size for _, size in windows) // TOK
    return pl.pallas_call(
        functools.partial(
            help_kernel, windows=windows, where=lambda i, y, z: jnp.where(y == 0, -1, NY * NZ)
        ),
        out_shape=(
            jax.ShapeDtypeStruct((8, ROWS), F32),
            jax.ShapeDtypeStruct((QH_DEV * 2 * FEAT + ROWS, HD), BF16),
        ),
        in_specs=[vmem] * (2 + len(pieces)),
        out_specs=(vmem,) * 2,
        scratch_shapes=[pltpu.VMEM(c.shape, c.dtype) for c in CARRY] + work_space(blocks),
        compiler_params=pltpu.CompilerParams(vmem_limit_bytes=VMEM),
        cost_estimate=pl.CostEstimate(flops=HELP_COST * 10**6, transcendentals=10**6, bytes_accessed=2**21),
    )(fkt, rows, *pieces)


def last_kernel(samples_ref, fkt_ref, rows_ref, *refs, where, windows):
    parts = len(windows)
    old, pieces, refs = refs[:4], tuple(zip(refs[4:4 + parts], windows)), refs[4 + parts:]
    sums_ref, packed_ref, phi_ref, numer_ref, denom_ref, student_ref, teacher_ref, square_ref, keep = refs[:9]
    carry = refs[9:13]
    take_in(fkt_ref, rows_ref, old, pieces, *refs[9:], where)
    best_ref, total_ref, accum_ref, state_ref = carry
    y, z = position()
    picked = samples_ref[y * NZ + z]
    for h in range(QH_DEV):
        rows = pl.ds(h * TOK, TOK)
        here = pl.ds(h * 2 * FEAT, 2 * FEAT)
        first = (state_ref[here, :HD] + packed_ref[here, :].astype(F32)).astype(BF16)
        state = jnp.concatenate([first, state_ref[here, HD:].astype(BF16)], axis=1)
        across = dot_nn(phi_ref[rows, :], state)
        more = sums_ref[pl.ds(2 + h // 2, 1), pl.ds((h % 2) * 2 * FEAT, 2 * FEAT)]
        more = dot_nt(phi_ref[rows, :], jnp.broadcast_to(more, (HD, 2 * FEAT)).astype(BF16))
        ratio = (numer_ref[rows, :] + across[:, :HD]) / (denom_ref[rows, :] + across[:, HD:] + more)
        ratio = ratio.astype(BF16)
        student_ref[h] = ratio
        keep[h] = ratio.astype(F32)
    best = best_ref[...]
    other = jnp.where(y == NY - 1, sums_ref[pl.ds(0, 1), :], MASKED)
    newtop = jnp.maximum(best, other)
    fade = jnp.exp2(best - newtop)
    rise = jnp.exp2(other - newtop)
    total = fade * total_ref[...] + rise * sums_ref[pl.ds(1, 1), :]
    squares = jnp.zeros((BLOCK, HD), F32)
    for h in range(QH_DEV):
        cols = slice(h * BLOCK, (h + 1) * BLOCK)
        added = packed_ref[pl.ds(QH_DEV * 2 * FEAT + h * HD, HD), :].astype(F32)
        mixed = (fade[:, cols] * accum_ref[:, cols] + rise[:, cols] * added) / total[:, cols]
        teacher = jnp.transpose(mixed)
        teacher_ref[h] = teacher
        gap = keep[h, pl.ds(pl.multiple_of(picked * BLOCK, BLOCK), BLOCK), :] - teacher
        squares = squares + gap * gap
    square_ref[...] = jnp.full(square_ref.shape, jnp.sum(squares), F32)


def last_part(samples, fkt, rows, carry, pieces, where, helped, phi, numer, denom, group):
    vmem = pl.BlockSpec(memory_space=pltpu.VMEM)
    return pl.pallas_call(
        functools.partial(last_kernel, where=where, windows=whole(pieces)),
        out_shape=(
            jax.ShapeDtypeStruct((QH_DEV, TOK, HD), BF16),
            jax.ShapeDtypeStruct((QH_DEV, BLOCK, HD), F32),
            jax.ShapeDtypeStruct((group, 1, 128), F32),
        ),
        in_specs=[pl.BlockSpec(memory_space=pltpu.SMEM)] + [vmem] * (11 + len(pieces)),
        out_specs=(vmem,) * 3,
        scratch_shapes=[pltpu.VMEM((QH_DEV, TOK, HD), F32)]
        + [pltpu.VMEM(c.shape, c.dtype) for c in CARRY]
        + work_space(sum(p.shape[0] for p in pieces) // TOK),
        compiler_params=pltpu.CompilerParams(vmem_limit_bytes=VMEM),
    )(samples, fkt, rows, *carry, *pieces, *helped, phi, numer, denom)


def join_kernel(k_ref, v_ref, own_ref):
    own_ref[:, :HD] = k_ref[...]
    own_ref[:, HD:] = v_ref[...]


def join(k, v):
    vmem = pl.BlockSpec(memory_space=pltpu.VMEM)
    return pl.pallas_call(
        join_kernel,
        out_shape=jax.ShapeDtypeStruct((TOK, 2 * HD), BF16),
        in_specs=[vmem] * 2,
        out_specs=vmem,
        compiler_params=pltpu.CompilerParams(vmem_limit_bytes=4 * 2**20),
    )(k, v)


def hold_kernel(x_ref, after_ref, out_ref):
    out_ref[...] = x_ref[...]


def hold(x, after):
    vmem = pl.BlockSpec(memory_space=pltpu.VMEM)
    return pl.pallas_call(
        hold_kernel,
        out_shape=jax.ShapeDtypeStruct(x.shape, x.dtype),
        in_specs=[vmem, pl.BlockSpec(memory_space=pl.ANY)],
        out_specs=vmem,
        compiler_params=pltpu.CompilerParams(vmem_limit_bytes=4 * 2**20),
    )(x, after)


def along_z(x, step):
    return lax.ppermute(x, "z", [(z, (z + step) % NZ) for z in range(NZ)])


def along_y(x, step, least=0):
    return lax.ppermute(x, "y", [(y, y + step) for y in range(NY) if least <= y and 0 <= y + step < NY])


def listed(*blocks):
    def place(block, y, z):
        back, step = block
        column = (y - back) * NZ + lax.rem(z + NZ - step, NZ)
        return column if back == 0 else jnp.where(y < back, NY * NZ, column)

    def where(i, y, z):
        if isinstance(i, int):
            return place(blocks[i], y, z)
        found = place(blocks[0], y, z)
        for n in range(1, len(blocks)):
            found = jnp.where(i == n, place(blocks[n], y, z), found)
        return found

    return where


def earlier(step):
    return ((1, step), (2, step))


def on_device(queries, keys, values, feat_q, feat_k, samples):
    group = lax.axis_size("y") * lax.axis_size("z") * lax.axis_size("head")
    k, v = (pltpu.with_memory_space_constraint(a[:, 0], pltpu.HBM) for a in (keys, values))
    own = join(k, v)
    far = [along_z(own, step) for step in (2, -2)]
    column = jnp.concatenate([along_y(own, 1), along_y(own, 2)], axis=0)
    near = [along_z(own, step) for step in (1, -1)]
    q = jnp.transpose(queries, (1, 0, 2))
    fkt = jnp.transpose(feat_k, (0, 2, 1))
    phi, numer, denom, rows, *carry = own_part(samples, column, q, k, v, feat_q, fkt)
    up = along_z(jnp.concatenate([column, far[0]], axis=0), 1)
    down = along_z(jnp.concatenate([far[1], column], axis=0), -1)
    carry = absorb(fkt, rows, carry, [column], listed(*earlier(0)))
    carry = absorb(fkt, rows, carry, near + far, listed((0, 1), (0, -1), (0, 2), (0, -2)))
    first = [up, down]
    half = TOK // 2
    asked = along_y(hold(rows, down), 1 - NY)
    helped = help_last_row(
        fkt, asked, [own, *near, *far, up, down],
        ((0, TOK),) * 5 + ((2 * TOK, TOK), (0, TOK)),
    )
    helped = [along_y(a, NY - 1) for a in helped]
    up, down = along_z(up[:-half], 1), along_z(down[half:], -1)
    carry = absorb(fkt, rows, carry, first, listed(*earlier(1), (0, 3), (0, -3), *earlier(-1)))
    second = [up, down]
    opposite = along_y(jnp.concatenate([up[-half:], down[:half]], axis=0), NY - 1)
    up, down = along_z(up[:-half], 1), along_z(down[half:], -1)
    carry = absorb(fkt, rows, carry, second, listed(*earlier(2), (0, 4), *earlier(-2)))
    third = [up, down]
    up, down = along_z(up[:TOK], 1), along_z(down[TOK:], -1)
    carry = absorb(fkt, rows, carry, third, listed(*earlier(3), *earlier(-3)))
    student, teacher, square = last_part(
        samples, fkt, rows, carry, [up, down, opposite], listed((1, 4), (2, 4), (3, 4)),
        helped, phi, numer, denom, group,
    )
    shared = lax.all_to_all(square, ("y", "z", "head"), 0, 0)
    loss = jnp.sum(shared[:, 0, 0]) / (group * BLOCK * QH_DEV * HD)
    return (
        jnp.transpose(student, (1, 0, 2)),
        jnp.transpose(teacher, (1, 0, 2))[None],
        loss,
    )


def solution(mesh):
    head = mesh.shape["head"]
    torus = Mesh(mesh.devices.reshape(NY, NZ, head), ("y", "z", "head"))
    seq = ("y", "z")
    in_specs = (
        P(seq, "head", None),
        P(seq, "head", None),
        P(seq, "head", None),
        P("head", None, None),
        P("head", None, None),
        P(),
    )
    out_specs = (P(seq, "head", None), P(seq, None, "head", None), P())
    return jax.shard_map(
        on_device, mesh=torus, in_specs=in_specs, out_specs=out_specs, check_vma=False
    )
```

```python
import functools

import jax
import jax.numpy as jnp
from jax import lax
from jax.experimental import pallas as pl
from jax.experimental.pallas import tpu as pltpu
from jax.sharding import Mesh, PartitionSpec as P

HD = 128
FEAT = 128
QH_DEV = 4
BLOCK = 128
TOK = 256
ROWS = QH_DEV * BLOCK
NY = 4
NZ = 8
MASKED = -1e30
COST = 10000
OWN_VMEM = 12 * 2**20
VMEM = 28 * 2**20
OWN_COST = 1000
F32 = jnp.float32
BF16 = jnp.bfloat16
LOG2E = 1.4426950408889634
SCORE_SCALE = LOG2E / HD**0.5


def dot_nn(a, b):
    return lax.dot_general(a, b, (((1,), (0,)), ((), ())), preferred_element_type=F32)


def dot_nt(a, b):
    return lax.dot_general(a, b, (((1,), (1,)), ((), ())), preferred_element_type=F32)


def dot_tn(a, b):
    return lax.dot_general(a, b, (((0,), (0,)), ((), ())), preferred_element_type=F32)


def both_softmax(logits, axis):
    up = jnp.exp(logits - jnp.max(logits, axis=axis, keepdims=True))
    down = jnp.exp(jnp.min(logits, axis=axis, keepdims=True) - logits)
    up = up * (1.0 / jnp.sum(up, axis=axis, keepdims=True))
    down = down * (1.0 / jnp.sum(down, axis=axis, keepdims=True))
    return jnp.concatenate([up, down], axis=axis).astype(BF16)


def position():
    return lax.axis_index("y"), lax.axis_index("z")


def own_kernel(samples_ref, q_ref, k_ref, v_ref, fq_ref, fkt_ref,
               phi_ref, numer_ref, denom_ref, rows_ref, best_ref, total_ref, accum_ref):
    y, z = position()
    picked = samples_ref[y * NZ + z]
    keys = k_ref[...]
    vals = v_ref[...]
    causal = lax.broadcasted_iota(jnp.int32, (TOK, TOK), 0) >= lax.broadcasted_iota(
        jnp.int32, (TOK, TOK), 1
    )
    for h in range(QH_DEV):
        rows = pl.ds(h * TOK, TOK)
        phi_q = both_softmax(dot_nn(q_ref[h], fq_ref[h]), 1)
        phi_k = both_softmax(dot_nt(fkt_ref[h], keys), 0)
        kernel = jnp.where(causal, dot_nn(phi_q, phi_k), 0.0)
        phi_ref[rows, :] = phi_q
        numer_ref[rows, :] = dot_nn(kernel.astype(BF16), vals)
        denom_ref[rows, :] = jnp.broadcast_to(jnp.sum(kernel, axis=1, keepdims=True), (TOK, HD))
        rows_ref[pl.ds(h * BLOCK, BLOCK), :] = q_ref[h, pl.ds(pl.multiple_of(picked * BLOCK, BLOCK), BLOCK), :]
    scores = dot_nt(keys, rows_ref[...]) * SCORE_SCALE
    place = picked * BLOCK + lax.rem(lax.broadcasted_iota(jnp.int32, scores.shape, 1), BLOCK)
    live = lax.broadcasted_iota(jnp.int32, scores.shape, 0) <= place
    scores = jnp.where(live, scores, MASKED)
    best = jnp.max(scores, axis=0, keepdims=True)
    weights = jnp.exp2(scores - best)
    best_ref[...] = best
    total_ref[...] = jnp.sum(weights, axis=0, keepdims=True)
    accum_ref[...] = dot_tn(vals, weights.astype(BF16))


def own_part(samples, q, k, v, fq, fkt):
    vmem = pl.BlockSpec(memory_space=pltpu.VMEM)
    return pl.pallas_call(
        own_kernel,
        out_shape=(
            jax.ShapeDtypeStruct((QH_DEV * TOK, 2 * FEAT), BF16),
            jax.ShapeDtypeStruct((QH_DEV * TOK, HD), F32),
            jax.ShapeDtypeStruct((QH_DEV * TOK, HD), F32),
            jax.ShapeDtypeStruct((ROWS, HD), BF16),
            jax.ShapeDtypeStruct((1, ROWS), F32),
            jax.ShapeDtypeStruct((1, ROWS), F32),
            jax.ShapeDtypeStruct((HD, ROWS), F32),
        ),
        in_specs=[pl.BlockSpec(memory_space=pltpu.SMEM)] + [vmem] * 5,
        out_specs=(vmem,) * 7,
        compiler_params=pltpu.CompilerParams(vmem_limit_bytes=OWN_VMEM),
        cost_estimate=pl.CostEstimate(flops=OWN_COST * 10**6, transcendentals=10**6, bytes_accessed=2**21),
    )(samples, q, k, v, fq, fkt)


def take_in(fkt_ref, rows_ref, old, pieces, best_ref, total_ref, accum_ref, state_ref,
            first_ref, second_ref, scores_ref, where):
    y, z = position()
    mine = y * NZ + z
    blocks = scores_ref.shape[0] // TOK
    live = [where(i, y, z) < mine for i in range(blocks)]
    some = functools.reduce(jnp.logical_or, live)
    if old[3] is None:
        state_ref[...] = jnp.zeros(state_ref.shape, F32)
    else:
        state_ref[...] = old[3][...]

    @pl.when(jnp.logical_not(some))
    def _():
        best_ref[...] = old[0][...]
        total_ref[...] = old[1][...]
        accum_ref[...] = old[2][...]

    def go(buffer, weights_ref, phi_ref):
        begin = 0
        for piece in pieces:
            buffer[pl.ds(begin, piece.shape[0]), :] = piece[...]
            begin += piece.shape[0]

        def span(i):
            return pl.ds(pl.multiple_of(i * TOK, TOK), TOK)

        def logits(i, to):
            keys = buffer[span(i), :HD]
            for h in range(QH_DEV):
                to[h] = dot_nt(fkt_ref[h], keys)

        def score(i, top):
            scores = dot_nt(buffer[span(i), :HD], rows_ref[...])
            scores_ref[span(i), :] = scores
            peak = jnp.max(scores.reshape(TOK // 8, 8, ROWS), axis=0)
            return jnp.maximum(top, jnp.where(where(i, y, z) < mine, peak, MASKED))

        def feature(i, out_of):
            keep = jnp.where(where(i, y, z) < mine, 1.0, 0.0).astype(F32)
            for h in range(QH_DEV):
                for half in range(2):
                    part = out_of[h, :, half * 128:(half + 1) * 128]
                    up = jnp.exp(part - jnp.max(part, axis=0, keepdims=True))
                    down = jnp.exp(jnp.min(part, axis=0, keepdims=True) - part)
                    up = up * (keep / jnp.sum(up, axis=0, keepdims=True))
                    down = down * (keep / jnp.sum(down, axis=0, keepdims=True))
                    to = pl.ds(pl.multiple_of(i * TOK, TOK) + half * 128, 128)
                    phi_ref[pl.ds(h * 2 * FEAT, FEAT), to] = up.astype(BF16)
                    phi_ref[pl.ds(h * 2 * FEAT + FEAT, FEAT), to] = down.astype(BF16)

        logits(0, first_ref)

        def two(j, top):
            i = 2 * j
            logits(i + 1, second_ref)
            feature(i, first_ref)
            top = score(i, top)
            logits(jnp.minimum(i + 2, blocks - 1), first_ref)
            feature(i + 1, second_ref)
            return score(i + 1, top)

        top = lax.fori_loop(0, blocks // 2, two, jnp.full((8, ROWS), MASKED, F32))
        if blocks % 2:
            feature(blocks - 1, first_ref)
            top = score(blocks - 1, top)
        best = old[0][...]
        newtop = jnp.maximum(best, jnp.max(top, axis=0, keepdims=True) * SCORE_SCALE)
        fade = jnp.exp2(best - newtop)
        best_ref[...] = newtop
        sums = jnp.zeros((8, ROWS), F32)
        ones = jnp.ones((blocks * TOK, HD), BF16)
        wide = jnp.concatenate([buffer[:, HD:], ones], axis=1)
        state_ref[...] = state_ref[...] + dot_nn(phi_ref[...], wide)
        for i in range(blocks):
            shift = jnp.where(live[i], newtop, -MASKED)
            weights = jnp.exp2(scores_ref[pl.ds(i * TOK, TOK), :] * SCORE_SCALE - shift)
            sums = sums + jnp.sum(weights.reshape(TOK // 8, 8, ROWS), axis=0)
            weights_ref[pl.ds(i * TOK, TOK), :] = weights.astype(BF16)
        total_ref[...] = fade * old[1][...] + jnp.sum(sums, axis=0, keepdims=True)
        accum_ref[...] = fade * old[2][...] + dot_tn(buffer[:, HD:], weights_ref[...])

    @pl.when(some)
    def _():
        pl.run_scoped(
            go,
            pltpu.VMEM((blocks * TOK, 2 * HD), BF16),
            pltpu.VMEM((blocks * TOK, ROWS), BF16),
            pltpu.VMEM((QH_DEV * 2 * FEAT, blocks * TOK), BF16),
        )


def work_space(blocks):
    return [
        pltpu.VMEM((QH_DEV, FEAT, TOK), F32),
        pltpu.VMEM((QH_DEV, FEAT, TOK), F32),
        pltpu.VMEM((blocks * TOK, ROWS), F32),
    ]


CARRY = (
    jax.ShapeDtypeStruct((1, ROWS), F32),
    jax.ShapeDtypeStruct((1, ROWS), F32),
    jax.ShapeDtypeStruct((HD, ROWS), F32),
    jax.ShapeDtypeStruct((QH_DEV * 2 * FEAT, 2 * HD), F32),
)


def absorb_kernel(fkt_ref, rows_ref, *refs, where, parts, fresh):
    carried = 3 if fresh else 4
    old = refs[:3] + ((None,) if fresh else (refs[3],))
    pieces = refs[carried:carried + parts]
    take_in(fkt_ref, rows_ref, old, pieces, *refs[carried + parts:], where)


def absorb(fkt, rows, carry, pieces, where):
    vmem = pl.BlockSpec(memory_space=pltpu.VMEM)
    fresh = len(carry) == 3
    return pl.pallas_call(
        functools.partial(absorb_kernel, where=where, parts=len(pieces), fresh=fresh),
        out_shape=CARRY,
        in_specs=[vmem] * (2 + len(carry) + len(pieces)),
        out_specs=(vmem,) * 4,
        scratch_shapes=work_space(sum(p.shape[0] for p in pieces) // TOK),
        compiler_params=pltpu.CompilerParams(vmem_limit_bytes=VMEM),
        cost_estimate=pl.CostEstimate(flops=COST * 10**6, transcendentals=10**6, bytes_accessed=2**21),
    )(fkt, rows, *carry, *pieces)


def last_kernel(samples_ref, fkt_ref, rows_ref, *refs, where, parts):
    old, pieces, refs = refs[:4], refs[4:4 + parts], refs[4 + parts:]
    phi_ref, numer_ref, denom_ref, student_ref, teacher_ref, square_ref, keep = refs[:7]
    carry = refs[7:11]
    take_in(fkt_ref, rows_ref, old, pieces, *refs[7:], where)
    total_ref, accum_ref, state_ref = carry[1:]
    y, z = position()
    picked = samples_ref[y * NZ + z]
    for h in range(QH_DEV):
        rows = pl.ds(h * TOK, TOK)
        state = state_ref[pl.ds(h * 2 * FEAT, 2 * FEAT), :].astype(BF16)
        across = dot_nn(phi_ref[rows, :], state)
        ratio = (numer_ref[rows, :] + across[:, :HD]) / (denom_ref[rows, :] + across[:, HD:])
        ratio = ratio.astype(BF16)
        student_ref[h] = ratio
        keep[h] = ratio.astype(F32)
    mixed = jnp.transpose(accum_ref[...] / total_ref[...])
    squares = jnp.zeros((BLOCK, HD), F32)
    for h in range(QH_DEV):
        teacher = mixed[h * BLOCK:(h + 1) * BLOCK]
        teacher_ref[h] = teacher
        gap = keep[h, pl.ds(pl.multiple_of(picked * BLOCK, BLOCK), BLOCK), :] - teacher
        squares = squares + gap * gap
    square_ref[...] = jnp.full(square_ref.shape, jnp.sum(squares), F32)


def last_part(samples, fkt, rows, carry, pieces, where, phi, numer, denom, group):
    vmem = pl.BlockSpec(memory_space=pltpu.VMEM)
    return pl.pallas_call(
        functools.partial(last_kernel, where=where, parts=len(pieces)),
        out_shape=(
            jax.ShapeDtypeStruct((QH_DEV, TOK, HD), BF16),
            jax.ShapeDtypeStruct((QH_DEV, BLOCK, HD), F32),
            jax.ShapeDtypeStruct((group, 1, 128), F32),
        ),
        in_specs=[pl.BlockSpec(memory_space=pltpu.SMEM)] + [vmem] * (9 + len(pieces)),
        out_specs=(vmem,) * 3,
        scratch_shapes=[pltpu.VMEM((QH_DEV, TOK, HD), F32)]
        + [pltpu.VMEM(c.shape, c.dtype) for c in CARRY]
        + work_space(sum(p.shape[0] for p in pieces) // TOK),
        compiler_params=pltpu.CompilerParams(vmem_limit_bytes=VMEM),
    )(samples, fkt, rows, *carry, *pieces, phi, numer, denom)


def spread_kernel(k_ref, v_ref, own_ref, wide_ref):
    pair = jnp.concatenate([k_ref[...], v_ref[...]], axis=1)
    own_ref[...] = pair
    for row in range(NY):
        wide_ref[row] = pair


def spread(k, v):
    vmem = pl.BlockSpec(memory_space=pltpu.VMEM)
    return pl.pallas_call(
        spread_kernel,
        out_shape=(
            jax.ShapeDtypeStruct((TOK, 2 * HD), BF16),
            jax.ShapeDtypeStruct((NY, TOK, 2 * HD), BF16),
        ),
        in_specs=[vmem] * 2,
        out_specs=(vmem,) * 2,
        compiler_params=pltpu.CompilerParams(vmem_limit_bytes=4 * 2**20),
    )(k, v)


def along_z(x, step):
    return lax.ppermute(x, "z", [(z, (z + step) % NZ) for z in range(NZ)])


def listed(*blocks):
    def place(block, y, z):
        row, step = block
        column = lax.rem(z + NZ - step, NZ)
        if row is None:
            return y * NZ + column
        return jnp.where(y == row, NY * NZ, row * NZ + column)

    def where(i, y, z):
        if isinstance(i, int):
            return place(blocks[i], y, z)
        found = place(blocks[0], y, z)
        for n in range(1, len(blocks)):
            found = jnp.where(i == n, place(blocks[n], y, z), found)
        return found

    return where


def earlier(step):
    return tuple((row, step) for row in range(NY - 1))


def on_device(queries, keys, values, feat_q, feat_k, samples):
    group = lax.axis_size("y") * lax.axis_size("z") * lax.axis_size("head")
    k, v = (pltpu.with_memory_space_constraint(a[:, 0], pltpu.HBM) for a in (keys, values))
    own, wide = spread(k, v)
    near = [along_z(own, step) for step in (1, -1)]
    far = [along_z(own, step) for step in (2, -2)]
    column = lax.all_to_all(wide, "y", 0, 0)
    column = column.reshape(NY * TOK, 2 * HD)[: (NY - 1) * TOK]
    q = jnp.transpose(queries, (1, 0, 2))
    fkt = jnp.transpose(feat_k, (0, 2, 1))
    phi, numer, denom, rows, *carry = own_part(samples, q, k, v, feat_q, fkt)
    up = along_z(jnp.concatenate([column, far[0]], axis=0), 1)
    down = along_z(jnp.concatenate([far[1], column], axis=0), -1)
    carry = absorb(fkt, rows, carry, [column], listed(*earlier(0)))
    carry = absorb(
        fkt, rows, carry, near + far, listed((None, 1), (None, -1), (None, 2), (None, -2))
    )
    first = [up, down]
    half = TOK // 2
    up, down = along_z(up[:-half], 1), along_z(down[half:], -1)
    carry = absorb(
        fkt, rows, carry, first,
        listed(*earlier(1), (None, 3), (None, -3), *earlier(-1)),
    )
    second = [up, down]
    up, down = along_z(up[:-half], 1), along_z(down[half:], -1)
    carry = absorb(fkt, rows, carry, second, listed(*earlier(2), (None, 4), *earlier(-2)))
    third = [up, down]
    half = up.shape[0] // 2
    up, down = along_z(up[:half], 1), along_z(down[half:], -1)
    carry = absorb(fkt, rows, carry, third, listed(*earlier(3), *earlier(-3)))
    student, teacher, square = last_part(
        samples, fkt, rows, carry, [up, down], listed(*earlier(4)), phi, numer, denom, group
    )
    shared = lax.all_to_all(square, ("y", "z", "head"), 0, 0)
    loss = jnp.sum(shared[:, 0, 0]) / (group * BLOCK * QH_DEV * HD)
    return (
        jnp.transpose(student, (1, 0, 2)),
        jnp.transpose(teacher, (1, 0, 2))[None],
        loss,
    )


def solution(mesh):
    head = mesh.shape["head"]
    torus = Mesh(mesh.devices.reshape(NY, NZ, head), ("y", "z", "head"))
    seq = ("y", "z")
    in_specs = (
        P(seq, "head", None),
        P(seq, "head", None),
        P(seq, "head", None),
        P("head", None, None),
        P("head", None, None),
        P(),
    )
    out_specs = (P(seq, "head", None), P(seq, None, "head", None), P())
    return jax.shard_map(
        on_device, mesh=torus, in_specs=in_specs, out_specs=out_specs, check_vma=False
    )
```

```python
import functools

import jax
import jax.numpy as jnp
from jax import lax
from jax.experimental import pallas as pl
from jax.experimental.pallas import tpu as pltpu
from jax.sharding import Mesh, PartitionSpec as P

HD = 128
FEAT = 128
QH_DEV = 4
BLOCK = 128
TOK = 256
ROWS = QH_DEV * BLOCK
NY = 4
NZ = 8
MASKED = -1e30
COST = 10000
OWN_VMEM = 12 * 2**20
VMEM = 28 * 2**20
OWN_COST = 1000
F32 = jnp.float32
BF16 = jnp.bfloat16
LOG2E = 1.4426950408889634
SCORE_SCALE = LOG2E / HD**0.5


def dot_nn(a, b):
    return lax.dot_general(a, b, (((1,), (0,)), ((), ())), preferred_element_type=F32)


def dot_nt(a, b):
    return lax.dot_general(a, b, (((1,), (1,)), ((), ())), preferred_element_type=F32)


def dot_tn(a, b):
    return lax.dot_general(a, b, (((0,), (0,)), ((), ())), preferred_element_type=F32)


def both_softmax(logits, axis):
    up = jnp.exp(logits - jnp.max(logits, axis=axis, keepdims=True))
    down = jnp.exp(jnp.min(logits, axis=axis, keepdims=True) - logits)
    up = up * (1.0 / jnp.sum(up, axis=axis, keepdims=True))
    down = down * (1.0 / jnp.sum(down, axis=axis, keepdims=True))
    return jnp.concatenate([up, down], axis=axis).astype(BF16)


def position():
    return lax.axis_index("y"), lax.axis_index("z")


def own_kernel(samples_ref, after_ref, q_ref, k_ref, v_ref, fq_ref, fkt_ref,
               phi_ref, numer_ref, denom_ref, rows_ref, best_ref, total_ref, accum_ref):
    y, z = position()
    picked = samples_ref[y * NZ + z]
    keys = k_ref[...]
    vals = v_ref[...]
    causal = lax.broadcasted_iota(jnp.int32, (TOK, TOK), 0) >= lax.broadcasted_iota(
        jnp.int32, (TOK, TOK), 1
    )
    for h in range(QH_DEV):
        rows = pl.ds(h * TOK, TOK)
        phi_q = both_softmax(dot_nn(q_ref[h], fq_ref[h]), 1)
        phi_k = both_softmax(dot_nt(fkt_ref[h], keys), 0)
        kernel = jnp.where(causal, dot_nn(phi_q, phi_k), 0.0)
        phi_ref[rows, :] = phi_q
        numer_ref[rows, :] = dot_nn(kernel.astype(BF16), vals)
        denom_ref[rows, :] = jnp.broadcast_to(jnp.sum(kernel, axis=1, keepdims=True), (TOK, HD))
        rows_ref[pl.ds(h * BLOCK, BLOCK), :] = q_ref[h, pl.ds(pl.multiple_of(picked * BLOCK, BLOCK), BLOCK), :]
    scores = dot_nt(keys, rows_ref[...]) * SCORE_SCALE
    place = picked * BLOCK + lax.rem(lax.broadcasted_iota(jnp.int32, scores.shape, 1), BLOCK)
    live = lax.broadcasted_iota(jnp.int32, scores.shape, 0) <= place
    scores = jnp.where(live, scores, MASKED)
    best = jnp.max(scores, axis=0, keepdims=True)
    weights = jnp.exp2(scores - best)
    best_ref[...] = best
    total_ref[...] = jnp.sum(weights, axis=0, keepdims=True)
    accum_ref[...] = dot_tn(vals, weights.astype(BF16))


def own_part(samples, after, q, k, v, fq, fkt):
    vmem = pl.BlockSpec(memory_space=pltpu.VMEM)
    return pl.pallas_call(
        own_kernel,
        out_shape=(
            jax.ShapeDtypeStruct((QH_DEV * TOK, 2 * FEAT), BF16),
            jax.ShapeDtypeStruct((QH_DEV * TOK, HD), F32),
            jax.ShapeDtypeStruct((QH_DEV * TOK, HD), F32),
            jax.ShapeDtypeStruct((ROWS, HD), BF16),
            jax.ShapeDtypeStruct((1, ROWS), F32),
            jax.ShapeDtypeStruct((1, ROWS), F32),
            jax.ShapeDtypeStruct((HD, ROWS), F32),
        ),
        in_specs=[pl.BlockSpec(memory_space=pltpu.SMEM), pl.BlockSpec(memory_space=pl.ANY)] + [vmem] * 5,
        out_specs=(vmem,) * 7,
        compiler_params=pltpu.CompilerParams(vmem_limit_bytes=OWN_VMEM),
        cost_estimate=pl.CostEstimate(flops=OWN_COST * 10**6, transcendentals=10**6, bytes_accessed=2**21),
    )(samples, after, q, k, v, fq, fkt)


def take_in(fkt_ref, rows_ref, old, pieces, best_ref, total_ref, accum_ref, state_ref,
            first_ref, second_ref, scores_ref, where):
    y, z = position()
    mine = y * NZ + z
    blocks = scores_ref.shape[0] // TOK
    live = [where(i, y, z) < mine for i in range(blocks)]
    some = functools.reduce(jnp.logical_or, live)
    if old[3] is None:
        state_ref[...] = jnp.zeros(state_ref.shape, F32)
    else:
        state_ref[...] = old[3][...]

    @pl.when(jnp.logical_not(some))
    def _():
        best_ref[...] = old[0][...]
        total_ref[...] = old[1][...]
        accum_ref[...] = old[2][...]

    def go(buffer, weights_ref, phi_ref):
        begin = 0
        for piece in pieces:
            buffer[pl.ds(begin, piece.shape[0]), :] = piece[...]
            begin += piece.shape[0]

        def span(i):
            return pl.ds(pl.multiple_of(i * TOK, TOK), TOK)

        def logits(i, to):
            keys = buffer[span(i), :HD]
            for h in range(QH_DEV):
                to[h] = dot_nt(fkt_ref[h], keys)

        def score(i, top):
            scores = dot_nt(buffer[span(i), :HD], rows_ref[...])
            scores_ref[span(i), :] = scores
            peak = jnp.max(scores.reshape(TOK // 8, 8, ROWS), axis=0)
            return jnp.maximum(top, jnp.where(where(i, y, z) < mine, peak, MASKED))

        def feature(i, out_of):
            keep = jnp.where(where(i, y, z) < mine, 1.0, 0.0).astype(F32)
            for h in range(QH_DEV):
                for half in range(2):
                    part = out_of[h, :, half * 128:(half + 1) * 128]
                    up = jnp.exp(part - jnp.max(part, axis=0, keepdims=True))
                    down = jnp.exp(jnp.min(part, axis=0, keepdims=True) - part)
                    up = up * (keep / jnp.sum(up, axis=0, keepdims=True))
                    down = down * (keep / jnp.sum(down, axis=0, keepdims=True))
                    to = pl.ds(pl.multiple_of(i * TOK, TOK) + half * 128, 128)
                    phi_ref[pl.ds(h * 2 * FEAT, FEAT), to] = up.astype(BF16)
                    phi_ref[pl.ds(h * 2 * FEAT + FEAT, FEAT), to] = down.astype(BF16)

        logits(0, first_ref)

        def two(j, top):
            i = 2 * j
            logits(i + 1, second_ref)
            feature(i, first_ref)
            top = score(i, top)
            logits(jnp.minimum(i + 2, blocks - 1), first_ref)
            feature(i + 1, second_ref)
            return score(i + 1, top)

        top = lax.fori_loop(0, blocks // 2, two, jnp.full((8, ROWS), MASKED, F32))
        if blocks % 2:
            feature(blocks - 1, first_ref)
            top = score(blocks - 1, top)
        best = old[0][...]
        newtop = jnp.maximum(best, jnp.max(top, axis=0, keepdims=True) * SCORE_SCALE)
        fade = jnp.exp2(best - newtop)
        best_ref[...] = newtop
        sums = jnp.zeros((8, ROWS), F32)
        ones = jnp.ones((blocks * TOK, HD), BF16)
        wide = jnp.concatenate([buffer[:, HD:], ones], axis=1)
        state_ref[...] = state_ref[...] + dot_nn(phi_ref[...], wide)
        for i in range(blocks):
            shift = jnp.where(live[i], newtop, -MASKED)
            weights = jnp.exp2(scores_ref[pl.ds(i * TOK, TOK), :] * SCORE_SCALE - shift)
            sums = sums + jnp.sum(weights.reshape(TOK // 8, 8, ROWS), axis=0)
            weights_ref[pl.ds(i * TOK, TOK), :] = weights.astype(BF16)
        total_ref[...] = fade * old[1][...] + jnp.sum(sums, axis=0, keepdims=True)
        accum_ref[...] = fade * old[2][...] + dot_tn(buffer[:, HD:], weights_ref[...])

    @pl.when(some)
    def _():
        pl.run_scoped(
            go,
            pltpu.VMEM((blocks * TOK, 2 * HD), BF16),
            pltpu.VMEM((blocks * TOK, ROWS), BF16),
            pltpu.VMEM((QH_DEV * 2 * FEAT, blocks * TOK), BF16),
        )


def work_space(blocks):
    return [
        pltpu.VMEM((QH_DEV, FEAT, TOK), F32),
        pltpu.VMEM((QH_DEV, FEAT, TOK), F32),
        pltpu.VMEM((blocks * TOK, ROWS), F32),
    ]


CARRY = (
    jax.ShapeDtypeStruct((1, ROWS), F32),
    jax.ShapeDtypeStruct((1, ROWS), F32),
    jax.ShapeDtypeStruct((HD, ROWS), F32),
    jax.ShapeDtypeStruct((QH_DEV * 2 * FEAT, 2 * HD), F32),
)


def absorb_kernel(fkt_ref, rows_ref, *refs, where, parts, fresh):
    carried = 3 if fresh else 4
    old = refs[:3] + ((None,) if fresh else (refs[3],))
    pieces = refs[carried:carried + parts]
    take_in(fkt_ref, rows_ref, old, pieces, *refs[carried + parts:], where)


def absorb(fkt, rows, carry, pieces, where):
    vmem = pl.BlockSpec(memory_space=pltpu.VMEM)
    fresh = len(carry) == 3
    return pl.pallas_call(
        functools.partial(absorb_kernel, where=where, parts=len(pieces), fresh=fresh),
        out_shape=CARRY,
        in_specs=[vmem] * (2 + len(carry) + len(pieces)),
        out_specs=(vmem,) * 4,
        scratch_shapes=work_space(sum(p.shape[0] for p in pieces) // TOK),
        compiler_params=pltpu.CompilerParams(vmem_limit_bytes=VMEM),
        cost_estimate=pl.CostEstimate(flops=COST * 10**6, transcendentals=10**6, bytes_accessed=2**21),
    )(fkt, rows, *carry, *pieces)


def last_kernel(samples_ref, fkt_ref, rows_ref, *refs, where, parts):
    old, pieces, refs = refs[:4], refs[4:4 + parts], refs[4 + parts:]
    phi_ref, numer_ref, denom_ref, student_ref, teacher_ref, square_ref, keep = refs[:7]
    carry = refs[7:11]
    take_in(fkt_ref, rows_ref, old, pieces, *refs[7:], where)
    total_ref, accum_ref, state_ref = carry[1:]
    y, z = position()
    picked = samples_ref[y * NZ + z]
    for h in range(QH_DEV):
        rows = pl.ds(h * TOK, TOK)
        state = state_ref[pl.ds(h * 2 * FEAT, 2 * FEAT), :].astype(BF16)
        across = dot_nn(phi_ref[rows, :], state)
        ratio = (numer_ref[rows, :] + across[:, :HD]) / (denom_ref[rows, :] + across[:, HD:])
        ratio = ratio.astype(BF16)
        student_ref[h] = ratio
        keep[h] = ratio.astype(F32)
    mixed = jnp.transpose(accum_ref[...] / total_ref[...])
    squares = jnp.zeros((BLOCK, HD), F32)
    for h in range(QH_DEV):
        teacher = mixed[h * BLOCK:(h + 1) * BLOCK]
        teacher_ref[h] = teacher
        gap = keep[h, pl.ds(pl.multiple_of(picked * BLOCK, BLOCK), BLOCK), :] - teacher
        squares = squares + gap * gap
    square_ref[...] = jnp.full(square_ref.shape, jnp.sum(squares), F32)


def last_part(samples, fkt, rows, carry, pieces, where, phi, numer, denom, group):
    vmem = pl.BlockSpec(memory_space=pltpu.VMEM)
    return pl.pallas_call(
        functools.partial(last_kernel, where=where, parts=len(pieces)),
        out_shape=(
            jax.ShapeDtypeStruct((QH_DEV, TOK, HD), BF16),
            jax.ShapeDtypeStruct((QH_DEV, BLOCK, HD), F32),
            jax.ShapeDtypeStruct((group, 1, 128), F32),
        ),
        in_specs=[pl.BlockSpec(memory_space=pltpu.SMEM)] + [vmem] * (9 + len(pieces)),
        out_specs=(vmem,) * 3,
        scratch_shapes=[pltpu.VMEM((QH_DEV, TOK, HD), F32)]
        + [pltpu.VMEM(c.shape, c.dtype) for c in CARRY]
        + work_space(sum(p.shape[0] for p in pieces) // TOK),
        compiler_params=pltpu.CompilerParams(vmem_limit_bytes=VMEM),
    )(samples, fkt, rows, *carry, *pieces, phi, numer, denom)


def spread_kernel(k_ref, v_ref, own_ref, wide_ref):
    pair = jnp.concatenate([k_ref[...], v_ref[...]], axis=1)
    own_ref[...] = pair
    for row in range(NY):
        wide_ref[row] = pair


def spread(k, v):
    vmem = pl.BlockSpec(memory_space=pltpu.VMEM)
    return pl.pallas_call(
        spread_kernel,
        out_shape=(
            jax.ShapeDtypeStruct((TOK, 2 * HD), BF16),
            jax.ShapeDtypeStruct((NY, TOK, 2 * HD), BF16),
        ),
        in_specs=[vmem] * 2,
        out_specs=(vmem,) * 2,
        compiler_params=pltpu.CompilerParams(vmem_limit_bytes=4 * 2**20),
    )(k, v)


def along_z(x, step):
    return lax.ppermute(x, "z", [(z, (z + step) % NZ) for z in range(NZ)])


def listed(*blocks):
    def place(block, y, z):
        row, step = block
        column = lax.rem(z + NZ - step, NZ)
        if row is None:
            return y * NZ + column
        return jnp.where(y == row, NY * NZ, row * NZ + column)

    def where(i, y, z):
        if isinstance(i, int):
            return place(blocks[i], y, z)
        found = place(blocks[0], y, z)
        for n in range(1, len(blocks)):
            found = jnp.where(i == n, place(blocks[n], y, z), found)
        return found

    return where


def earlier(step):
    return tuple((row, step) for row in range(NY - 1))


def on_device(queries, keys, values, feat_q, feat_k, samples):
    group = lax.axis_size("y") * lax.axis_size("z") * lax.axis_size("head")
    k, v = (pltpu.with_memory_space_constraint(a[:, 0], pltpu.HBM) for a in (keys, values))
    own, wide = spread(k, v)
    near = [along_z(own, step) for step in (1, -1)]
    far = [along_z(own, step) for step in (2, -2)]
    column = lax.all_to_all(wide, "y", 0, 0)
    column = column.reshape(NY * TOK, 2 * HD)[: (NY - 1) * TOK]
    q = jnp.transpose(queries, (1, 0, 2))
    fkt = jnp.transpose(feat_k, (0, 2, 1))
    phi, numer, denom, rows, *carry = own_part(
        samples, column, q, k, v, feat_q, fkt
    )
    up, down = along_z(column, 1), along_z(column, -1)
    carry = absorb(fkt, rows, carry, [column], listed(*earlier(0)))
    carry = absorb(
        fkt, rows, carry, near + far, listed((None, 1), (None, -1), (None, 2), (None, -2))
    )
    first = [up, down]
    up = along_z(jnp.concatenate([up, far[0]], axis=0), 1)
    down = along_z(jnp.concatenate([far[1], down], axis=0), -1)
    carry = absorb(fkt, rows, carry, first, listed(*earlier(1), *earlier(-1)))
    second = [up, down]
    half = TOK // 2
    up, down = along_z(up[:-half], 1), along_z(down[half:], -1)
    carry = absorb(
        fkt, rows, carry, second,
        listed(*earlier(2), (None, 3), (None, -3), *earlier(-2)),
    )
    third = [up, down]
    half = 3 * TOK // 2
    up, down = along_z(up[:half], 1), along_z(down[-half:], -1)
    carry = absorb(fkt, rows, carry, third, listed(*earlier(3), (None, 4), *earlier(-3)))
    student, teacher, square = last_part(
        samples, fkt, rows, carry, [up, down], listed(*earlier(4)), phi, numer, denom, group
    )
    shared = lax.all_to_all(square, ("y", "z", "head"), 0, 0)
    loss = jnp.sum(shared[:, 0, 0]) / (group * BLOCK * QH_DEV * HD)
    return (
        jnp.transpose(student, (1, 0, 2)),
        jnp.transpose(teacher, (1, 0, 2))[None],
        loss,
    )


def solution(mesh):
    head = mesh.shape["head"]
    torus = Mesh(mesh.devices.reshape(NY, NZ, head), ("y", "z", "head"))
    seq = ("y", "z")
    in_specs = (
        P(seq, "head", None),
        P(seq, "head", None),
        P(seq, "head", None),
        P("head", None, None),
        P("head", None, None),
        P(),
    )
    out_specs = (P(seq, "head", None), P(seq, None, "head", None), P())
    return jax.shard_map(
        on_device, mesh=torus, in_specs=in_specs, out_specs=out_specs, check_vma=False
    )
```
